256 devices in a mesh: ctx: 64 (over x_lo, z, y), head: 4 (over x_hi, core).
Axes of the slice: x: 4 (x_hi: 2, x_lo: 2; x = x_hi * 2 + x_lo), y: 4, z: 8, core: 2. Of those that a mesh axis runs over, the one named last changes fastest.
Arguments:
- query_local: bfloat16 [12288, 5120], P(('ctx', 'head')), may hold values from -6 to 6
- key_local: bfloat16 [12288, 1024], P(('ctx', 'head')), may hold values from -6 to 6
- value_local: bfloat16 [12288, 1024], P(('ctx', 'head')), may hold values from -6 to 6
- stretch_labels: int32 [12288], replicated, may hold values from 0 to 31, never falling along the last dimension, each value on 1 to 768 neighbouring positions
- query_global: bfloat16 [12288, 5120], P(('ctx', 'head')), may hold values from -5 to 5
- key_global: bfloat16 [12288, 1024], P(('ctx', 'head')), may hold values from -5 to 5
- value_global: bfloat16 [12288, 1024], P(('ctx', 'head')), may hold values from -6 to 6
Outputs:
- local_heads: bfloat16 [12288, 5120], P(('ctx', 'head'))
- global_heads: bfloat16 [12288, 5120], P(('ctx', 'head'))
The draws below stay inside these ranges and needn't reach their ends.
Inputs may be any that keep to these rules, and one draw needn't show every extreme that they name: `stretch_labels`: stretches are runs of consecutive tokens; numbers never fall; each stretch has 1 to 768 tokens and some stretch has exactly 768.
All inputs are finite; a program needn't handle non-finite values.
Results may differ from the reference program's by a relative error of at most 0.0059.
Values may be sent and summed in bfloat16 or wider, within the bound.
A program may use at most 128 MiB of HBM per device.

```python
import math
import jax
import jax.numpy as jnp
import numpy as np
from jax import lax

HEAD = 128
QH = 40
KVH = 8
TOK_DEV = 192
TOKENS = 12288
STRETCH = 768


def drawn(key):
    query_key = jax.random.fold_in(key, 11)
    key_stream = jax.random.fold_in(key, 12)
    query_width = QH * HEAD
    key_width = KVH * HEAD
    query_draw = jnp.clip(2.5 * jax.random.normal(query_key, (TOKENS, query_width), jnp.float32), -5.0, 5.0)
    key_draw = jnp.clip(jax.random.normal(key_stream, (TOKENS, key_width), jnp.float32), -4.0, 4.0)
    return (query_draw, key_draw)


def draw_query_global(key, part):
    return drawn(key)[0].astype(jnp.bfloat16)


def draw_key_global(key, part):
    return drawn(key)[1].astype(jnp.bfloat16)


def shard_levels(own_key, shape, pieces, smallest, largest):
    def one(position, parts):
        steps = jax.random.uniform(jax.random.fold_in(jax.random.fold_in(own_key, 6), position), (parts,), jnp.float32, smallest / len(pieces), largest / len(pieces))
        return jnp.repeat(jnp.exp(steps), shape[position] // parts).reshape((-1,) + (1,) * (len(shape) - position - 1))

    level = one(*pieces[0])
    for cut in pieces[1:]:
        level = level * one(*cut)
    return level


def profile(amount, total, limit, skew):
    weights = [(1 << 20) // math.isqrt(grade ** skew) + 1 for grade in range(2, amount + 1)]
    rest, counts = total - limit - (amount - 1), [1] * (amount - 1)
    while rest > 0:
        movable = [i for i in range(amount - 1) if counts[i] < limit]
        whole, budget = sum([weights[i] for i in movable]), rest
        for i in movable:
            addition = min(limit - counts[i], max(1, budget * weights[i] // whole), rest)
            counts[i] = counts[i] + addition
            rest = rest - addition
    return np.array([limit] + counts)


def uneven(rng, number_of, total, limit, slope):
    if number_of == 2:
        one = jax.random.randint(rng, (), max(1, total - limit), min(limit, total - 1) + 1)
        return jnp.stack([one, total - one])
    tallies = jnp.asarray(profile(number_of, total, limit, slope), jnp.int32)
    couples = (number_of - 1) // 2
    source_of, taker = tallies[1:1 + 2 * couples:2], tallies[2:2 + 2 * couples:2]
    margin = jnp.minimum(source_of - 1, limit - taker)
    moved = jax.random.randint(jax.random.fold_in(rng, 1), (couples,), 0, 1 << 20) % (margin + 1)
    tallies = tallies.at[1:1 + 2 * couples:2].set(source_of - moved).at[2:2 + 2 * couples:2].set(taker + moved)
    return tallies[jax.random.permutation(jax.random.fold_in(rng, 2), number_of)]


def bell_draw(stream_key, dims, scale, reach, shards=(), kind=jnp.bfloat16):
    drawn = jax.random.normal(stream_key, dims, jnp.float32) * scale
    if len(shards) > 0:
        drawn = shard_levels(stream_key, dims, shards, -0.22, 0.18) * drawn
    return jnp.clip(drawn, min=-reach, max=reach).astype(kind)


def setup_inputs(seed: int = 0) -> dict:
    arg_keys = jax.random.split(jax.random.key(seed), 8)
    query_local = bell_draw(arg_keys[0], (TOKENS, QH * HEAD), 1.0, 6.0, ((0, 256),))
    key_local = bell_draw(arg_keys[1], (TOKENS, KVH * HEAD), 1.0, 6.0, ((0, 256),))
    value_local = bell_draw(arg_keys[2], (TOKENS, KVH * HEAD), 1.0, 6.0, ((0, 256),))
    stretch_labels = jnp.searchsorted(jnp.cumsum(uneven(arg_keys[3], TOKENS // (2 * TOK_DEV), TOKENS, STRETCH, 2)), jnp.arange(TOKENS), side="right").astype(jnp.int32)
    query_global = draw_query_global(jax.random.fold_in(arg_keys[7], 71), 0)
    key_global = draw_key_global(jax.random.fold_in(arg_keys[7], 71), 0)
    value_global = bell_draw(arg_keys[6], (TOKENS, KVH * HEAD), 1.0, 6.0, ((0, 256),))
    return dict(query_local=query_local, key_local=key_local, value_local=value_local, stretch_labels=stretch_labels, query_global=query_global, key_global=key_global, value_global=value_global)


rope_base = 500000.0
norm_epsilon = 1e-06
temper_floor = 8192
temper_slope = 0.1
masked_score = -1e+30

def rotate(tensor, positions):
    head_width = tensor.shape[-1]
    half_width = head_width // 2
    frequency = rope_base ** (-(jnp.arange(half_width, dtype=jnp.float32) * 2.0 / head_width))
    angles = positions.astype(jnp.float32)[:, None] * frequency[None, :]
    extra_dims = tensor.ndim - 2
    angles = angles.reshape((angles.shape[0],) + (1,) * extra_dims + (half_width,))
    cosine = jnp.cos(angles)
    sine_part = jnp.sin(angles)
    first_part = tensor[..., :half_width]
    second_part = tensor[..., half_width:]
    return jnp.concatenate([first_part * cosine - second_part * sine_part, first_part * sine_part + second_part * cosine], axis=-1)

def normalize(tensor):
    return tensor * lax.rsqrt(lax.optimization_barrier(jnp.mean(tensor * tensor, axis=-1, keepdims=True)) + norm_epsilon)

def tempering(positions):
    return 1.0 + temper_slope * jnp.log(((positions + 1) // temper_floor + 1).astype(jnp.float32))

def reference(query_local, key_local, value_local, stretch_labels, query_global, key_global, value_global):
    length = query_local.shape[0]
    key_heads = key_local.shape[1] // HEAD
    group_size = query_local.shape[1] // (key_heads * HEAD)
    scaling = HEAD ** (-0.5)
    positions = jnp.arange(length, dtype=jnp.int32)
    query_shape = (length, key_heads, group_size, HEAD)
    key_shape = (length, key_heads, HEAD)
    queries = normalize(rotate(query_local.astype(jnp.float32).reshape(query_shape), positions)).astype(jnp.bfloat16)
    keys_normed = normalize(rotate(key_local.astype(jnp.float32).reshape(key_shape), positions)).astype(jnp.bfloat16)
    queries = lax.optimization_barrier(queries).astype(jnp.float32)
    keys_normed = lax.optimization_barrier(keys_normed).astype(jnp.float32)
    values_local = value_local.astype(jnp.float32).reshape(key_shape)
    block_rows = 256 if length % 256 == 0 else length
    reach_rows = STRETCH
    padded_keys = jnp.concatenate([jnp.zeros((reach_rows, key_heads, HEAD), jnp.float32), keys_normed], axis=0)
    padded_values = jnp.concatenate([jnp.zeros((reach_rows, key_heads, HEAD), jnp.float32), values_local], axis=0)
    padded_labels = jnp.concatenate([jnp.full((reach_rows,), -1, jnp.int32), stretch_labels.astype(jnp.int32)], axis=0)

    def local_block(anchor):
        query_block = lax.dynamic_slice_in_dim(queries, anchor, block_rows, 0)
        query_ids = lax.dynamic_slice_in_dim(stretch_labels.astype(jnp.int32), anchor, block_rows, 0)
        query_pos = anchor + jnp.arange(block_rows, dtype=jnp.int32)
        key_block = lax.dynamic_slice_in_dim(padded_keys, anchor, reach_rows + block_rows, 0)
        value_block = lax.dynamic_slice_in_dim(padded_values, anchor, reach_rows + block_rows, 0)
        key_ids = lax.dynamic_slice_in_dim(padded_labels, anchor, reach_rows + block_rows, 0)
        key_pos = anchor - reach_rows + jnp.arange(reach_rows + block_rows, dtype=jnp.int32)
        allowed = (key_ids[None, :] == query_ids[:, None]) & (key_pos[None, :] <= query_pos[:, None])
        scores = jnp.einsum('qhgd,khd->hgqk', query_block, key_block) * scaling
        weights = jnp.where(allowed[None, None], jnp.exp(scores), 0.0)
        totals = lax.optimization_barrier(jnp.sum(weights, axis=-1))
        rounded = lax.optimization_barrier(weights.astype(jnp.bfloat16)).astype(jnp.float32)
        weighted = jnp.einsum('hgqk,khd->qhgd', rounded, value_block)
        return (weighted / jnp.transpose(totals, (2, 0, 1))[..., None]).astype(jnp.bfloat16)
    anchors = jnp.arange(0, length, block_rows, dtype=jnp.int32)
    local_heads = lax.map(local_block, anchors).reshape(length, -1)
    query_rows = query_global.astype(jnp.float32).reshape(query_shape)
    key_rows = key_global.astype(jnp.float32).reshape(key_shape)
    value_rows = value_global.astype(jnp.float32).reshape(key_shape)
    temper_scale = tempering(positions) * scaling
    global_rows = 128 if length % 128 == 0 else length

    def global_block(anchor):
        query_block = lax.dynamic_slice_in_dim(query_rows, anchor, global_rows, 0)
        query_pos = anchor + jnp.arange(global_rows, dtype=jnp.int32)
        block_scale = lax.dynamic_slice_in_dim(temper_scale, anchor, global_rows, 0)
        scores = jnp.einsum('qhgd,khd->hgqk', query_block, key_rows) * block_scale[None, None, :, None]
        allowed = positions[None, :] <= query_pos[:, None]
        scores = jnp.where(allowed[None, None], scores, masked_score)
        row_peak = lax.optimization_barrier(jnp.max(scores, axis=-1))
        powers = jnp.where(allowed[None, None], jnp.exp(scores - row_peak[..., None]), 0.0)
        totals = lax.optimization_barrier(jnp.sum(powers, axis=-1))
        rounded = lax.optimization_barrier(powers.astype(jnp.bfloat16)).astype(jnp.float32)
        weighted = jnp.einsum('hgqk,khd->qhgd', rounded, value_rows)
        return (weighted / jnp.transpose(totals, (2, 0, 1))[..., None]).astype(jnp.bfloat16)
    global_anchors = jnp.arange(0, length, global_rows, dtype=jnp.int32)
    global_heads = lax.map(global_block, global_anchors).reshape(length, -1)
    return (local_heads, global_heads)
```

```python
import functools

import jax
import jax.numpy as jnp
from jax import lax
from jax.experimental import pallas as pl
from jax.experimental.pallas import tpu as pltpu
from jax.sharding import PartitionSpec as P

HEAD = 128
GROUP = 5
WIDE = GROUP * HEAD
TOK = 192
OWN = 48
NZ, NY = 8, 4
ROWS = GROUP * TOK
CHUNK = NY * TOK
SPAN = 4
KEYS = (SPAN + 1) * TOK
TILE = 320

rope_base = 500000.0
norm_epsilon = 1e-06
temper_shift = 13
temper_slope = 0.1
masked_score = -1e30
log2e = 1.4426950408889634
scaling = HEAD ** (-0.5)

MESH = pl.DeviceIdType.MESH
KG, VG, KL, VL, QL, QG, OL, OG = range(8)


def tiled(x, n):
    return jnp.concatenate([x] * n, axis=1)


def kernel(
    ql_ref, kl_ref, vl_hbm, qg_hbm, kg_hbm, vg_hbm, cos_ref, sin_ref, kid_ref, qid_ref,
    ol_hbm, og_hbm,
    kv, lkv, qg_buf, lq_buf, nq, nk, qs, m_ref, acc, og_buf, ol_buf, bias,
    a2a_send, a2a_recv, ring_send, ring_recv, halo_send, halo_recv,
):
    ctx = lax.axis_index("ctx")
    head = lax.axis_index("head")
    x_lo = ctx // 32
    c = ctx % 32
    z = c // NY
    y = c % NY
    g = x_lo * 4 + head
    flip = 31 - c

    def at(row, member):
        return {"ctx": (member // 4) * 32 + row, "head": member % 4}

    def line(row):
        return {"ctx": x_lo * 32 + row, "head": head}

    def wrap(v, n):
        return lax.rem(v + n, n)

    barrier = pltpu.get_barrier_semaphore()

    def greet(device):
        pl.semaphore_signal(barrier, inc=1, device_id=device, device_id_type=MESH)

    @pl.loop(0, 8)
    def _(t):
        greet(at(flip, t))

    @pl.loop(1, 8)
    def _(t):
        greet(at(c, g ^ t))

    for s in (1, -1):
        greet(line(z * NY + wrap(y + s, NY)))
        greet(line(wrap(z + s, NZ) * NY + y))

    @pl.loop(1, SPAN + 1)
    def _(t):
        greet(line(lax.rem(c + t, 32)))
        greet(line(lax.rem(c - t + 32, 32)))

    pl.semaphore_wait(barrier, 27)

    my_rows = pl.ds(head * OWN, OWN)

    def exchange_refs(kind, target):
        narrow = pl.ds(pl.multiple_of(target * HEAD, HEAD), HEAD)
        wide = pl.ds(pl.multiple_of(target * WIDE, HEAD), WIDE)
        mine = pl.ds(pl.multiple_of(g * WIDE, HEAD), WIDE)
        their = pl.ds(lax.rem(target, 4) * OWN, OWN)
        if kind == KG:
            return kg_hbm.at[:, narrow], kv.at[x_lo, z, y, 0, my_rows, :]
        if kind == VG:
            return vg_hbm.at[:, narrow], kv.at[x_lo, z, y, 1, my_rows, :]
        if kind == KL:
            return nk.at[:, narrow], lkv.at[x_lo, SPAN, 0, my_rows, :]
        if kind == VL:
            return vl_hbm.at[:, narrow], lkv.at[x_lo, SPAN, 1, my_rows, :]
        if kind == QL:
            return nq.at[:, wide], lq_buf.at[x_lo, my_rows, :]
        if kind == QG:
            return qg_hbm.at[:, wide], qg_buf.at[x_lo, my_rows, :]
        if kind == OL:
            return ol_buf.at[target // 4, their, :], ol_hbm.at[:, mine]
        return og_buf.at[target // 4, their, :], og_hbm.at[:, mine]

    def exchange(kind, d):
        target = g ^ d
        src, dst = exchange_refs(kind, target)
        if kind == QG:
            row = jnp.where(x_lo == 0, c, flip)
        elif kind == OG:
            row = jnp.where(target < 4, c, flip)
        else:
            row = c
        return pltpu.make_async_remote_copy(
            src_ref=src,
            dst_ref=dst,
            send_sem=a2a_send.at[kind, d],
            recv_sem=a2a_recv.at[kind, g],
            device_id=at(row, target),
            device_id_type=MESH,
        )

    def exchange_own(kind):
        src, dst = exchange_refs(kind, g)
        return pltpu.make_async_copy(src, dst, a2a_recv.at[kind, g])

    def send(kind):
        if kind in (QG, OG):

            @pl.when(x_lo == 0)
            def _():
                exchange_own(kind).start()

            @pl.when(x_lo == 1)
            def _():
                exchange(kind, 0).start()
        else:
            exchange_own(kind).start()

        @pl.loop(1, 8)
        def _(d):
            exchange(kind, d).start()

    def sent(kind):
        if kind in (QG, OG):

            @pl.when(x_lo == 1)
            def _():
                exchange(kind, 0).wait_send()

        @pl.loop(1, 8)
        def _(d):
            exchange(kind, d).wait_send()

    def received(kind):
        @pl.loop(0, 8)
        def _(t):
            _, dst = exchange_refs(kind, g)
            pltpu.make_async_copy(dst, dst, a2a_recv.at[kind, t]).wait()

    def hop(number, ref, device):
        return pltpu.make_async_remote_copy(
            src_ref=ref,
            dst_ref=ref,
            send_sem=ring_send.at[number],
            recv_sem=ring_recv.at[number],
            device_id=device,
            device_id_type=MESH,
        )

    def y_next(s):
        return line(z * NY + wrap(y + s, NY))

    def z_next(s):
        return line(wrap(z + s, NZ) * NY + y)

    def early_y(step, s):
        if step == 1:
            ref = kv.at[0, z, y]
        else:
            ref = kv.at[0, z, wrap(y - s, NY), 0 if s == 1 else 1]
        return hop(2 * (step - 1) + (s == 1), ref, y_next(s))

    def early_z(step, s):
        chunk = wrap(z - s * (step - 1), NZ)
        if step < 4:
            ref = kv.at[0, chunk]
        else:
            ref = kv.at[0, chunk, :, 0 if s == 1 else 1]
        return hop(4 + 2 * (step - 1) + (s == 1), ref, z_next(s))

    def late_z(step, s):
        chunk = wrap(z - s * (step - 1), NZ)
        if step < 4:
            ref = kv.at[1, chunk, y]
        else:
            ref = kv.at[1, chunk, y, 0 if s == 1 else 1]
        return hop(12 + 2 * (step - 1) + (s == 1), ref, z_next(s))

    def late_y(step, s):
        if step == 1:
            ref = kv.at[1, :, y]
        else:
            ref = kv.at[1, :, wrap(y - s, NY), 0 if s == 1 else 1]
        return hop(20 + 2 * (step - 1) + (s == 1), ref, y_next(s))

    def begin(family, step):
        for s in (1, -1):
            family(step, s).start()

    def arrived(family, step):
        for s in (1, -1):
            family(step, s).wait_recv()

    def left(family, steps):
        for step in range(1, steps + 1):
            for s in (1, -1):
                family(step, s).wait_send()

    def halo(d, e):
        row = lax.rem(c + d, 32)
        other = jnp.where(c + d >= 32, 1 - e, e)
        return pltpu.make_async_remote_copy(
            src_ref=lkv.at[e, SPAN],
            dst_ref=lkv.at[other, SPAN - d],
            send_sem=halo_send.at[d - 1, e],
            recv_sem=halo_recv.at[d - 1, other],
            device_id=line(row),
            device_id_type=MESH,
        )

    def normalized(x):
        x = x.astype(jnp.float32)
        r = x * cos_ref[...] + pltpu.roll(x, HEAD // 2, 1) * sin_ref[...]
        mean = jnp.mean(r * r, axis=-1, keepdims=True)
        return (r * lax.rsqrt(mean + norm_epsilon)).astype(jnp.bfloat16)

    send(KG)
    send(VG)
    for h in range(8):
        cols = slice(h * HEAD, (h + 1) * HEAD)
        nk[:, cols] = normalized(kl_ref[:, cols])
    received(KG)
    received(VG)
    begin(late_z, 1)
    begin(early_y, 1)
    send(KL)
    send(VL)
    send(QG)

    @pl.loop(0, 8)
    def _(t):
        for h in range(GROUP):
            cols = pl.ds(pl.multiple_of(t * WIDE + h * HEAD, HEAD), HEAD)
            nq[:, cols] = normalized(ql_ref[:, cols])

    send(QL)
    arrived(early_y, 1)
    begin(early_y, 2)
    arrived(late_z, 1)
    begin(late_z, 2)
    received(KL)
    received(VL)

    @pl.loop(1, SPAN + 1)
    def _(d):
        halo(d, 0).start()
        halo(d, 1).start()

    arrived(early_y, 2)
    begin(early_z, 1)
    arrived(late_z, 2)
    begin(late_z, 3)

    received(QG)
    m_ref[...] = jnp.full(m_ref.shape, masked_score, jnp.float32)
    acc[...] = jnp.zeros(acc.shape, jnp.float32)

    @pl.loop(0, 2)
    def _(e):
        block = jnp.where(e == 0, c, 63 - c)
        pos = block * TOK + lax.broadcasted_iota(jnp.int32, (TOK, HEAD), 0)
        level = lax.shift_right_logical(pos + 1, temper_shift) + 1
        temper = 1.0 + temper_slope * jnp.log(level.astype(jnp.float32))
        factor = temper * (scaling * log2e)
        for h in range(GROUP):
            x = qg_buf[e, :, h * HEAD : (h + 1) * HEAD].astype(jnp.float32) * factor
            high = x.astype(jnp.bfloat16)
            low = (x - high.astype(jnp.float32)).astype(jnp.bfloat16)
            qs[e, h * TOK : (h + 1) * TOK, :] = jnp.concatenate([high, low], axis=1)

    arrived(late_z, 3)
    begin(late_z, 4)

    received(QL)

    @pl.loop(1, SPAN + 1)
    def _(d):
        halo(d, 0).wait_recv()
        halo(d, 1).wait_recv()

    arrived(late_z, 4)
    begin(late_y, 1)

    @pl.loop(0, 2)
    def _(e):
        block = e * 32 + c
        row_pos = lax.broadcasted_iota(jnp.int32, (TOK, KEYS), 0) + SPAN * TOK
        key_pos = lax.broadcasted_iota(jnp.int32, (TOK, KEYS), 1)
        allowed = (qid_ref[e] == kid_ref[e]) & (key_pos <= row_pos)
        bias[...] = jnp.where(allowed, 0.0, masked_score)
        k = lkv[e, :, 0].reshape(KEYS, HEAD)
        v = lkv[e, :, 1].reshape(KEYS, HEAD)
        va = jnp.concatenate([v, jnp.ones((KEYS, HEAD), jnp.bfloat16)], axis=1)
        for h in range(GROUP):
            cols = slice(h * HEAD, (h + 1) * HEAD)
            s = lax.dot_general(
                lq_buf[e, :, cols], k, (((1,), (1,)), ((), ())),
                preferred_element_type=jnp.float32,
            )
            p = jnp.exp2(s * (scaling * log2e) + bias[...]).astype(jnp.bfloat16)
            o = jnp.dot(p, va, preferred_element_type=jnp.float32)
            ol_buf[e, :, cols] = (o[:, :HEAD] / o[:, HEAD:]).astype(jnp.bfloat16)

    send(OL)

    def unit(eq, ek, chunk, offset=None):
        k = kv[ek, chunk, :, 0].reshape(CHUNK, HEAD)
        v = kv[ek, chunk, :, 1].reshape(CHUNK, HEAD)
        kk = jnp.concatenate([k, k], axis=1)
        va = jnp.concatenate([v, jnp.ones((CHUNK, HEAD), jnp.bfloat16)], axis=1)
        for t in range(ROWS // TILE):
            rows = pl.ds(t * TILE, TILE)
            s = lax.dot_general(
                qs[eq, rows, :], kk, (((1,), (1,)), ((), ())),
                preferred_element_type=jnp.float32,
            )
            if offset is not None:
                r = t * TILE + lax.broadcasted_iota(jnp.int32, (TILE, HEAD), 0)
                for h in range(GROUP - 1, 0, -1):
                    r = jnp.where(r >= h * TOK, r - h * TOK, r)
                limit = tiled(r + offset, CHUNK // HEAD)
                key = lax.broadcasted_iota(jnp.int32, (TILE, CHUNK), 1)
                s = jnp.where(key <= limit, s, masked_score)
            before = m_ref[eq, rows, :]
            peak = jnp.maximum(before, jnp.max(s, axis=1, keepdims=True))
            factor = jnp.exp2(before - peak)
            p = jnp.exp2(s - tiled(peak, CHUNK // HEAD)).astype(jnp.bfloat16)
            acc[eq, rows, :] = acc[eq, rows, :] * tiled(factor, 2) + jnp.dot(
                p, va, preferred_element_type=jnp.float32
            )
            m_ref[eq, rows, :] = peak

    @pl.loop(0, 24)
    def _(j):
        @pl.when(j == 2)
        def _():
            arrived(early_z, 1)
            begin(early_z, 2)

        @pl.when(j == 6)
        def _():
            arrived(early_z, 2)
            begin(early_z, 3)

        @pl.when(j == 10)
        def _():
            arrived(early_z, 3)
            begin(early_z, 4)
            arrived(late_y, 1)
            begin(late_y, 2)

        @pl.when(j == 14)
        def _():
            arrived(early_z, 4)

        @pl.when(j == 16)
        def _():
            arrived(late_y, 2)

        i = j // 2
        away = (i + 1) // 2
        near = lax.rem(z + jnp.where(lax.rem(i, 2) == 1, 8 - away, away), NZ)
        late_keys = j >= 16
        chunk = jnp.where(late_keys, j - 16, near)
        eq = jnp.where(late_keys | (lax.rem(j, 2) == 0), 1, 0)
        ek = jnp.where(late_keys, 1, 0)
        do = jnp.where(late_keys, chunk < 7 - z, (eq == 1) | (chunk < z))

        @pl.when(do)
        def _():
            unit(eq, ek, chunk)

    @pl.loop(0, 2)
    def _(e):
        unit(e, e, jnp.where(e == 0, z, 7 - z), TOK * jnp.where(e == 0, y, 3 - y))
        for h in range(GROUP):
            o = acc[e, h * TOK : (h + 1) * TOK, :]
            og_buf[e, :, h * HEAD : (h + 1) * HEAD] = (o[:, :HEAD] / o[:, HEAD:]).astype(
                jnp.bfloat16
            )

    send(OG)
    for kind in (KG, VG, KL, VL, QL, QG, OL):
        sent(kind)
    left(early_y, 2)
    left(early_z, 4)
    left(late_z, 4)
    left(late_y, 2)

    @pl.loop(1, SPAN + 1)
    def _(d):
        halo(d, 0).wait_send()
        halo(d, 1).wait_send()

    received(OL)
    received(OG)
    sent(OG)


def shards(
    query_local, key_local, value_local, stretch_labels, query_global, key_global, value_global
):
    ctx = lax.axis_index("ctx")
    head = lax.axis_index("head")
    c = ctx % 32
    positions = (ctx * TOK + head * OWN + jnp.arange(OWN, dtype=jnp.int32)).astype(jnp.float32)
    half = HEAD // 2
    frequency = rope_base ** (-(jnp.arange(half, dtype=jnp.float32) * 2.0 / HEAD))
    angles = positions[:, None] * frequency[None, :]
    cosine, sine = jnp.cos(angles), jnp.sin(angles)
    cosine = jnp.concatenate([cosine, cosine], axis=1)
    sine = jnp.concatenate([-sine, sine], axis=1)
    padded = jnp.concatenate([jnp.full((SPAN * TOK,), -1, jnp.int32), stretch_labels])
    kid = jnp.stack(
        [lax.dynamic_slice_in_dim(padded, (32 * e + c) * TOK, KEYS, 0) for e in range(2)]
    )
    qid = kid[:, SPAN * TOK :].reshape(2, TOK, 1)
    kid = kid.reshape(2, 1, KEYS)
    any_space = pl.BlockSpec(memory_space=pl.ANY)
    vmem = pl.BlockSpec(memory_space=pltpu.VMEM)
    bf16, f32 = jnp.bfloat16, jnp.float32
    out = jax.ShapeDtypeStruct(query_local.shape, bf16)
    return pl.pallas_call(
        kernel,
        out_shape=(out, out),
        in_specs=[vmem, vmem] + [any_space] * 4 + [vmem] * 4,
        out_specs=(any_space, any_space),
        scratch_shapes=[
            pltpu.VMEM((2, NZ, NY, 2, TOK, HEAD), bf16),
            pltpu.VMEM((2, SPAN + 1, 2, TOK, HEAD), bf16),
            pltpu.VMEM((2, TOK, WIDE), bf16),
            pltpu.VMEM((2, TOK, WIDE), bf16),
            pltpu.VMEM((OWN, 8 * WIDE), bf16),
            pltpu.VMEM((OWN, 8 * HEAD), bf16),
            pltpu.VMEM((2, ROWS, 2 * HEAD), bf16),
            pltpu.VMEM((2, ROWS, HEAD), f32),
            pltpu.VMEM((2, ROWS, 2 * HEAD), f32),
            pltpu.VMEM((2, TOK, WIDE), bf16),
            pltpu.VMEM((2, TOK, WIDE), bf16),
            pltpu.VMEM((TOK, KEYS), f32),
            pltpu.SemaphoreType.DMA((8, 8)),
            pltpu.SemaphoreType.DMA((8, 8)),
            pltpu.SemaphoreType.DMA((24,)),
            pltpu.SemaphoreType.DMA((24,)),
            pltpu.SemaphoreType.DMA((SPAN, 2)),
            pltpu.SemaphoreType.DMA((SPAN, 2)),
        ],
        compiler_params=pltpu.CompilerParams(
            collective_id=0, has_side_effects=True, vmem_limit_bytes=48 << 20
        ),
    )(
        query_local, key_local, value_local, query_global, key_global, value_global,
        cosine, sine, kid, qid,
    )


def solution(mesh):
    rows = P(("ctx", "head"), None)
    return jax.shard_map(
        shards,
        mesh=mesh,
        in_specs=(rows, rows, rows, P(), rows, rows, rows),
        out_specs=(rows, rows),
        check_vma=False,
    )
```

```python
import functools

import jax
import jax.numpy as jnp
from jax import lax
from jax.experimental import pallas as pl
from jax.experimental.pallas import tpu as pltpu
from jax.sharding import PartitionSpec as P

HEAD = 128
GROUP = 5
WIDE = GROUP * HEAD
TOK = 192
OWN = 48
NZ, NY = 8, 4
ROWS = GROUP * TOK
CHUNK = NY * TOK
SPAN = 4
KEYS = (SPAN + 1) * TOK
TILE = 320

rope_base = 500000.0
norm_epsilon = 1e-06
temper_shift = 13
temper_slope = 0.1
masked_score = -1e30
log2e = 1.4426950408889634
scaling = HEAD ** (-0.5)

MESH = pl.DeviceIdType.MESH
KG, VG, KL, VL, QL, QG, OL, OG = range(8)


def tiled(x, n):
    return jnp.concatenate([x] * n, axis=1)


def kernel(
    ql_hbm, kl_hbm, vl_hbm, qg_hbm, kg_hbm, vg_hbm, cos_ref, sin_ref, kid_ref, qid_ref,
    ol_hbm, og_hbm,
    ql_ref, kl_ref, kv, lkv, qg_buf, lq_buf, nq, nk, qs, m_ref, acc, og_buf, ol_buf, bias,
    a2a_send, a2a_recv, ring_send, ring_recv, halo_send, halo_recv, load_sem,
):
    ctx = lax.axis_index("ctx")
    head = lax.axis_index("head")
    x_lo = ctx // 32
    c = ctx % 32
    z = c // NY
    y = c % NY
    g = x_lo * 4 + head

    def at(row, member):
        return {"ctx": (member // 4) * 32 + row, "head": member % 4}

    def line(row):
        return {"ctx": x_lo * 32 + row, "head": head}

    def wrap(v, n):
        return lax.rem(v + n, n)

    barrier = pltpu.get_barrier_semaphore()

    def greet(device):
        pl.semaphore_signal(barrier, inc=1, device_id=device, device_id_type=MESH)

    @pl.loop(1, 8)
    def _(t):
        greet(at(c, g ^ t))

    for s in (1, -1):
        greet(line(z * NY + wrap(y + s, NY)))
        greet(line(wrap(z + s, NZ) * NY + y))

    @pl.loop(1, SPAN + 1)
    def _(t):
        greet(line(lax.rem(c + t, 32)))
        greet(line(lax.rem(c - t + 32, 32)))

    load_k = pltpu.make_async_copy(kl_hbm, kl_ref, load_sem.at[0])
    load_q = pltpu.make_async_copy(ql_hbm, ql_ref, load_sem.at[1])
    load_k.start()
    load_q.start()
    pl.semaphore_wait(barrier, 19)

    my_rows = pl.ds(head * OWN, OWN)

    def exchange_refs(kind, target):
        narrow = pl.ds(pl.multiple_of(target * HEAD, HEAD), HEAD)
        wide = pl.ds(pl.multiple_of(target * WIDE, HEAD), WIDE)
        mine = pl.ds(pl.multiple_of(g * WIDE, HEAD), WIDE)
        their = pl.ds(lax.rem(target, 4) * OWN, OWN)
        if kind == KG:
            return kg_hbm.at[:, narrow], kv.at[x_lo, z, y, 0, my_rows, :]
        if kind == VG:
            return vg_hbm.at[:, narrow], kv.at[x_lo, z, y, 1, my_rows, :]
        if kind == KL:
            return nk.at[:, narrow], lkv.at[x_lo, SPAN, 0, my_rows, :]
        if kind == VL:
            return vl_hbm.at[:, narrow], lkv.at[x_lo, SPAN, 1, my_rows, :]
        if kind == QL:
            return nq.at[:, wide], lq_buf.at[x_lo, my_rows, :]
        if kind == QG:
            return qg_hbm.at[:, wide], qg_buf.at[x_lo, my_rows, :]
        if kind == OL:
            return ol_buf.at[target // 4, their, :], ol_hbm.at[:, mine]
        return og_buf.at[target // 4, their, :], og_hbm.at[:, mine]

    def exchange(kind, d):
        target = g ^ d
        src, dst = exchange_refs(kind, target)
        return pltpu.make_async_remote_copy(
            src_ref=src,
            dst_ref=dst,
            send_sem=a2a_send.at[kind, d],
            recv_sem=a2a_recv.at[kind, g],
            device_id=at(c, target),
            device_id_type=MESH,
        )

    def exchange_own(kind):
        src, dst = exchange_refs(kind, g)
        return pltpu.make_async_copy(src, dst, a2a_recv.at[kind, g])

    def send(kind):
        exchange_own(kind).start()

        @pl.loop(1, 8)
        def _(d):
            exchange(kind, d).start()

    def send_global(e):
        @pl.loop(0, 4)
        def _(h):
            d = g ^ (4 * e + h)

            @pl.when(d == 0)
            def _():
                exchange_own(OG).start()

            @pl.when(d != 0)
            def _():
                exchange(OG, d).start()

    def sent(kind):
        @pl.loop(1, 8)
        def _(d):
            exchange(kind, d).wait_send()

    def received(kind):
        @pl.loop(0, 8)
        def _(t):
            _, dst = exchange_refs(kind, g)
            pltpu.make_async_copy(dst, dst, a2a_recv.at[kind, t]).wait()

    def hop(number, ref, device):
        return pltpu.make_async_remote_copy(
            src_ref=ref,
            dst_ref=ref,
            send_sem=ring_send.at[number],
            recv_sem=ring_recv.at[number],
            device_id=device,
            device_id_type=MESH,
        )

    def y_next(s):
        return line(z * NY + wrap(y + s, NY))

    def z_next(s):
        return line(wrap(z + s, NZ) * NY + y)

    def near(i):
        return wrap(z + (-((i + 1) // 2) if i % 2 else i // 2), NZ)

    def early_y(step, s):
        if step == 1:
            ref = kv.at[0, z, y]
        else:
            ref = kv.at[0, z, wrap(y - s, NY), 0 if s == 1 else 1]
        return hop(2 * (step - 1) + (s == 1), ref, y_next(s))

    def early_first(n, s):
        ref = kv.at[0, z, lax.rem(y + (0, 3, 1, 2)[n], NY)]
        return hop(18 + 2 * n + (s == 1), ref, z_next(s))

    def early_z(step, s):
        ref = kv.at[0, wrap(z - s * (step - 1), NZ)]
        return hop(4 + 2 * (step - 2) + (s == 1), ref, z_next(s))

    def late_z(step, s):
        ref = kv.at[1, wrap(z - s * (step - 1), NZ), y]
        return hop(10 + 2 * (step - 1) + (s == 1), ref, z_next(s))

    def late_first(i, s):
        return hop(26 + 2 * i + (s == 1), kv.at[1, near(i), y], y_next(s))

    def late_second(i, s):
        ref = kv.at[1, near(i), wrap(y - s, NY), 0 if s == 1 else 1]
        return hop(42 + 2 * i + (s == 1), ref, y_next(s))

    def ways(family, step):
        return (-1,) if family in (early_z, late_z) and step == 4 else (1, -1)

    def begin(family, *steps):
        for step in steps:
            for s in ways(family, step):
                family(step, s).start()

    def arrived(family, *steps):
        for step in steps:
            for s in ways(family, step):
                family(step, s).wait_recv()

    def left(family, *steps):
        for step in steps:
            for s in ways(family, step):
                family(step, s).wait_send()

    def halo(d, e):
        row = lax.rem(c + d, 32)
        other = jnp.where(c + d >= 32, 1 - e, e)
        return pltpu.make_async_remote_copy(
            src_ref=lkv.at[e, SPAN],
            dst_ref=lkv.at[other, SPAN - d],
            send_sem=halo_send.at[d - 1, e],
            recv_sem=halo_recv.at[d - 1, other],
            device_id=line(row),
            device_id_type=MESH,
        )

    def normalized(x):
        x = x.astype(jnp.float32)
        r = x * cos_ref[...] + pltpu.roll(x, HEAD // 2, 1) * sin_ref[...]
        mean = jnp.mean(r * r, axis=-1, keepdims=True)
        return (r * lax.rsqrt(mean + norm_epsilon)).astype(jnp.bfloat16)

    send(KG)
    send(VG)
    load_k.wait()
    for h in range(8):
        cols = slice(h * HEAD, (h + 1) * HEAD)
        nk[:, cols] = normalized(kl_ref[:, cols])
    load_q.wait()

    @pl.loop(0, 8)
    def _(t):
        for h in range(GROUP):
            cols = pl.ds(pl.multiple_of(t * WIDE + h * HEAD, HEAD), HEAD)
            nq[:, cols] = normalized(ql_ref[:, cols])

    m_ref[...] = jnp.full(m_ref.shape, masked_score, jnp.float32)
    acc[...] = jnp.zeros(acc.shape, jnp.float32)
    received(KG)
    received(VG)
    begin(late_z, 1)
    begin(early_y, 1)
    begin(early_first, 0)
    begin(late_first, 0)
    send(QG)
    arrived(early_y, 1)
    begin(early_y, 2)
    begin(early_first, 1, 2)
    arrived(late_z, 1)
    begin(late_z, 2)
    begin(late_first, 1, 2)
    arrived(early_y, 2)
    begin(early_first, 3)
    send(KL)
    send(VL)
    arrived(late_z, 2)
    begin(late_z, 3)
    begin(late_first, 3, 4)
    received(QG)

    @pl.loop(0, 2)
    def _(e):
        block = e * 32 + c
        pos = block * TOK + lax.broadcasted_iota(jnp.int32, (TOK, HEAD), 0)
        level = lax.shift_right_logical(pos + 1, temper_shift) + 1
        temper = 1.0 + temper_slope * jnp.log(level.astype(jnp.float32))
        factor = temper * (scaling * log2e)
        for h in range(GROUP):
            x = qg_buf[e, :, h * HEAD : (h + 1) * HEAD].astype(jnp.float32) * factor
            high = x.astype(jnp.bfloat16)
            low = (x - high.astype(jnp.float32)).astype(jnp.bfloat16)
            qs[e, h * TOK : (h + 1) * TOK, :] = jnp.concatenate([high, low], axis=1)

    def local_attention():
        received(QL)

        @pl.loop(1, SPAN + 1)
        def _(d):
            halo(d, 0).wait_recv()
            halo(d, 1).wait_recv()

        @pl.loop(0, 2)
        def _(e):
            row_pos = lax.broadcasted_iota(jnp.int32, (TOK, KEYS), 0) + SPAN * TOK
            key_pos = lax.broadcasted_iota(jnp.int32, (TOK, KEYS), 1)
            allowed = (qid_ref[e] == kid_ref[e]) & (key_pos <= row_pos)
            bias[...] = jnp.where(allowed, 0.0, masked_score)
            k = lkv[e, :, 0].reshape(KEYS, HEAD)
            v = lkv[e, :, 1].reshape(KEYS, HEAD)
            va = jnp.concatenate([v, jnp.ones((KEYS, HEAD), jnp.bfloat16)], axis=1)
            for h in range(GROUP):
                cols = slice(h * HEAD, (h + 1) * HEAD)
                s = lax.dot_general(
                    lq_buf[e, :, cols], k, (((1,), (1,)), ((), ())),
                    preferred_element_type=jnp.float32,
                )
                p = jnp.exp2(s * (scaling * log2e) + bias[...]).astype(jnp.bfloat16)
                o = jnp.dot(p, va, preferred_element_type=jnp.float32)
                ol_buf[e, :, cols] = (o[:, :HEAD] / o[:, HEAD:]).astype(jnp.bfloat16)

        send(OL)

    def unit(eq, ek, zs, ys, start=None, slope=None):
        k = jnp.concatenate([kv[ek, zs[n], ys[n], 0] for n in range(4)], axis=0)
        v = jnp.concatenate([kv[ek, zs[n], ys[n], 1] for n in range(4)], axis=0)
        kk = jnp.concatenate([k, k], axis=1)
        va = jnp.concatenate([v, jnp.ones((CHUNK, HEAD), jnp.bfloat16)], axis=1)
        for t in range(ROWS // TILE):
            rows = pl.ds(t * TILE, TILE)
            s = lax.dot_general(
                qs[eq, rows, :], kk, (((1,), (1,)), ((), ())),
                preferred_element_type=jnp.float32,
            )
            if start is not None:
                r = t * TILE + lax.broadcasted_iota(jnp.int32, (TILE, HEAD), 0)
                for h in range(GROUP - 1, 0, -1):
                    r = jnp.where(r >= h * TOK, r - h * TOK, r)
                limit = tiled(r * slope + start, CHUNK // HEAD)
                key = lax.broadcasted_iota(jnp.int32, (TILE, CHUNK), 1)
                s = jnp.where(key <= limit, s, masked_score)
            before = m_ref[eq, rows, :]
            peak = jnp.maximum(before, jnp.max(s, axis=1, keepdims=True))
            factor = jnp.exp2(before - peak)
            p = jnp.exp2(s - tiled(peak, CHUNK // HEAD)).astype(jnp.bfloat16)
            acc[eq, rows, :] = acc[eq, rows, :] * tiled(factor, 2) + jnp.dot(
                p, va, preferred_element_type=jnp.float32
            )
            m_ref[eq, rows, :] = peak

    def finish(e):
        for h in range(GROUP):
            o = acc[e, h * TOK : (h + 1) * TOK, :]
            og_buf[e, :, h * HEAD : (h + 1) * HEAD] = (o[:, :HEAD] / o[:, HEAD:]).astype(
                jnp.bfloat16
            )
        send_global(e)

    def service_1():
        arrived(late_z, 3)
        begin(late_z, 4)
        begin(late_first, 5, 6)
        received(KL)
        received(VL)

        @pl.loop(1, SPAN + 1)
        def _(d):
            halo(d, 0).start()
            halo(d, 1).start()

        send(QL)
        arrived(early_first, 0, 1, 2, 3)
        begin(early_z, 2)

    def service_2():
        arrived(late_z, 4)
        begin(late_first, 7)

    def service_3():
        for i in range(5):
            arrived(late_first, i)
            begin(late_second, i)

    def service_4():
        arrived(early_z, 2)
        begin(early_z, 3)
        for i in range(5, 8):
            arrived(late_first, i)
            begin(late_second, i)

    def service_8():
        arrived(early_z, 3)
        begin(early_z, 4)

    def service_10():
        local_attention()
        arrived(early_z, 4)

    def service_11():
        finish(0)
        arrived(late_second, *range(8))

    services = {
        1: service_1,
        2: service_2,
        3: service_3,
        4: service_4,
        8: service_8,
        10: service_10,
        11: service_11,
    }

    @pl.loop(0, 24)
    def _(j):
        pair = j // 2
        second = lax.rem(j, 2)
        for at_pair, action in services.items():
            pl.when(j == 2 * at_pair)(action)

        column = (pair == 3) | (pair == 6) | (pair == 7) | (pair == 11)
        i = jnp.where(pair < 3, pair, jnp.where(pair < 6, pair - 1, pair - 3))
        away = (i + 1) // 2
        chunk = lax.rem(z + jnp.where(lax.rem(i, 2) == 1, 8 - away, away), NZ)
        turn = jnp.where(pair == 3, 0, jnp.where(pair == 6, 3, jnp.where(pair == 7, 1, 2)))
        y_col = lax.rem(y + turn, NY)
        z_rel = z - 4 * second

        early_query = jnp.logical_not(column) & (second == 1)
        eq = jnp.where(early_query, 0, 1)
        ek = jnp.where(column, 1, 0)
        do = jnp.where(column, z_rel >= 0, (second == 0) | (chunk <= z))
        masked = jnp.where(column, z_rel <= 3, (second == 1) & (chunk == z))
        slope = jnp.where(column & (y_col != y), 0, 1)
        start = jnp.where(
            column,
            z_rel * TOK + jnp.where(y_col < y, TOK - 1, jnp.where(y_col == y, 0, -1)),
            y * TOK,
        )
        zs = [jnp.where(column, 4 * second + n, chunk) for n in range(4)]
        ys = [jnp.where(column, y_col, n) for n in range(4)]

        @pl.when(do & jnp.logical_not(masked))
        def _():
            unit(eq, ek, zs, ys)

        @pl.when(do & masked)
        def _():
            unit(eq, ek, zs, ys, start, slope)

    finish(1)
    for kind in (KG, VG, KL, VL, QL, QG, OL):
        sent(kind)
    left(early_y, 1, 2)
    left(early_first, 0, 1, 2, 3)
    left(early_z, 2, 3, 4)
    left(late_z, 1, 2, 3, 4)
    left(late_first, *range(8))
    left(late_second, *range(8))

    @pl.loop(1, SPAN + 1)
    def _(d):
        halo(d, 0).wait_send()
        halo(d, 1).wait_send()

    received(OL)
    received(OG)
    sent(OG)


def shards(
    query_local, key_local, value_local, stretch_labels, query_global, key_global, value_global
):
    ctx = lax.axis_index("ctx")
    head = lax.axis_index("head")
    c = ctx % 32
    positions = (ctx * TOK + head * OWN + jnp.arange(OWN, dtype=jnp.int32)).astype(jnp.float32)
    half = HEAD // 2
    frequency = rope_base ** (-(jnp.arange(half, dtype=jnp.float32) * 2.0 / HEAD))
    angles = positions[:, None] * frequency[None, :]
    cosine, sine = jnp.cos(angles), jnp.sin(angles)
    cosine = jnp.concatenate([cosine, cosine], axis=1)
    sine = jnp.concatenate([-sine, sine], axis=1)
    padded = jnp.concatenate([jnp.full((SPAN * TOK,), -1, jnp.int32), stretch_labels])
    kid = jnp.stack(
        [lax.dynamic_slice_in_dim(padded, (32 * e + c) * TOK, KEYS, 0) for e in range(2)]
    )
    qid = kid[:, SPAN * TOK :].reshape(2, TOK, 1)
    kid = kid.reshape(2, 1, KEYS)
    any_space = pl.BlockSpec(memory_space=pl.ANY)
    vmem = pl.BlockSpec(memory_space=pltpu.VMEM)
    bf16, f32 = jnp.bfloat16, jnp.float32
    out = jax.ShapeDtypeStruct(query_local.shape, bf16)
    return pl.pallas_call(
        kernel,
        out_shape=(out, out),
        in_specs=[any_space] * 6 + [vmem] * 4,
        out_specs=(any_space, any_space),
        scratch_shapes=[
            pltpu.VMEM((OWN, 8 * WIDE), bf16),
            pltpu.VMEM((OWN, 8 * HEAD), bf16),
            pltpu.VMEM((2, NZ, NY, 2, TOK, HEAD), bf16),
            pltpu.VMEM((2, SPAN + 1, 2, TOK, HEAD), bf16),
            pltpu.VMEM((2, TOK, WIDE), bf16),
            pltpu.VMEM((2, TOK, WIDE), bf16),
            pltpu.VMEM((OWN, 8 * WIDE), bf16),
            pltpu.VMEM((OWN, 8 * HEAD), bf16),
            pltpu.VMEM((2, ROWS, 2 * HEAD), bf16),
            pltpu.VMEM((2, ROWS, HEAD), f32),
            pltpu.VMEM((2, ROWS, 2 * HEAD), f32),
            pltpu.VMEM((2, TOK, WIDE), bf16),
            pltpu.VMEM((2, TOK, WIDE), bf16),
            pltpu.VMEM((TOK, KEYS), f32),
            pltpu.SemaphoreType.DMA((8, 8)),
            pltpu.SemaphoreType.DMA((8, 8)),
            pltpu.SemaphoreType.DMA((58,)),
            pltpu.SemaphoreType.DMA((58,)),
            pltpu.SemaphoreType.DMA((SPAN, 2)),
            pltpu.SemaphoreType.DMA((SPAN, 2)),
            pltpu.SemaphoreType.DMA((2,)),
        ],
        compiler_params=pltpu.CompilerParams(
            collective_id=0, has_side_effects=True, vmem_limit_bytes=62 << 20
        ),
    )(
        query_local, key_local, value_local, query_global, key_global, value_global,
        cosine, sine, kid, qid,
    )


def solution(mesh):
    rows = P(("ctx", "head"), None)
    return jax.shard_map(
        shards,
        mesh=mesh,
        in_specs=(rows, rows, rows, P(), rows, rows, rows),
        out_specs=(rows, rows),
        check_vma=False,
    )
```

```python
import functools

import jax
import jax.numpy as jnp
from jax import lax
from jax.experimental import pallas as pl
from jax.experimental.pallas import tpu as pltpu
from jax.sharding import PartitionSpec as P

HEAD = 128
GROUP = 5
WIDE = GROUP * HEAD
TOK = 192
OWN = 48
NZ, NY = 8, 4
ROWS = GROUP * TOK
CHUNK = NY * TOK
SPAN = 4
KEYS = (SPAN + 1) * TOK
TILE = 320

rope_base = 500000.0
norm_epsilon = 1e-06
temper_shift = 13
temper_slope = 0.1
masked_score = -1e30
log2e = 1.4426950408889634
scaling = HEAD ** (-0.5)

MESH = pl.DeviceIdType.MESH
KG, VG, KL, VL, QL, QG, OL, OG = range(8)


def tiled(x, n):
    return jnp.concatenate([x] * n, axis=1)


def kernel(
    ql_hbm, kl_hbm, vl_hbm, qg_hbm, kg_hbm, vg_hbm, cos_ref, sin_ref, label_hbm,
    ol_hbm, og_hbm,
    ql_ref, kl_ref, labels, kv, lkv, qg_buf, lq_buf, nq, nk, qs, m_ref, acc, og_buf, ol_buf, bias,
    a2a_send, a2a_recv, ring_send, ring_recv, halo_send, halo_recv, load_sem,
):
    ctx = lax.axis_index("ctx")
    head = lax.axis_index("head")
    x_lo = ctx // 32
    c = ctx % 32
    z = c // NY
    y = c % NY
    g = x_lo * 4 + head

    def at(row, member):
        return {"ctx": (member // 4) * 32 + row, "head": member % 4}

    def line(row):
        return {"ctx": x_lo * 32 + row, "head": head}

    def wrap(v, n):
        return lax.rem(v + n, n)

    barrier = pltpu.get_barrier_semaphore()

    def greet(device):
        pl.semaphore_signal(barrier, inc=1, device_id=device, device_id_type=MESH)

    @pl.loop(1, 8)
    def _(t):
        greet(at(c, g ^ t))

    for s in (1, -1):
        greet(line(z * NY + wrap(y + s, NY)))
        greet(line(wrap(z + s, NZ) * NY + y))

    load_k = pltpu.make_async_copy(kl_hbm, kl_ref, load_sem.at[0])
    load_q = pltpu.make_async_copy(ql_hbm, ql_ref, load_sem.at[1])
    labels[:8, :] = jnp.full((8, HEAD), -1, jnp.int32)
    labels[104:, :] = jnp.full((8, HEAD), -1, jnp.int32)
    load_l = pltpu.make_async_copy(label_hbm, labels.at[8:104, :], load_sem.at[2])
    load_l.start()
    load_k.start()
    load_q.start()
    pl.semaphore_wait(barrier, 11)

    my_rows = pl.ds(head * OWN, OWN)

    def exchange_refs(kind, target):
        narrow = pl.ds(pl.multiple_of(target * HEAD, HEAD), HEAD)
        wide = pl.ds(pl.multiple_of(target * WIDE, HEAD), WIDE)
        mine = pl.ds(pl.multiple_of(g * WIDE, HEAD), WIDE)
        their = pl.ds(lax.rem(target, 4) * OWN, OWN)
        if kind == KG:
            return kg_hbm.at[:, narrow], kv.at[x_lo, z, y, 0, my_rows, :]
        if kind == VG:
            return vg_hbm.at[:, narrow], kv.at[x_lo, z, y, 1, my_rows, :]
        if kind == KL:
            return nk.at[:, narrow], lkv.at[x_lo, SPAN, 0, my_rows, :]
        if kind == VL:
            return vl_hbm.at[:, narrow], lkv.at[x_lo, SPAN, 1, my_rows, :]
        if kind == QL:
            return nq.at[:, wide], lq_buf.at[x_lo, my_rows, :]
        if kind == QG:
            return qg_hbm.at[:, wide], qg_buf.at[x_lo, my_rows, :]
        if kind == OL:
            return ol_buf.at[target // 4, their, :], ol_hbm.at[:, mine]
        return og_buf.at[target // 4, their, :], og_hbm.at[:, mine]

    def exchange(kind, d):
        target = g ^ d
        src, dst = exchange_refs(kind, target)
        return pltpu.make_async_remote_copy(
            src_ref=src,
            dst_ref=dst,
            send_sem=a2a_send.at[kind, d],
            recv_sem=a2a_recv.at[kind, g],
            device_id=at(c, target),
            device_id_type=MESH,
        )

    def exchange_own(kind):
        src, dst = exchange_refs(kind, g)
        return pltpu.make_async_copy(src, dst, a2a_recv.at[kind, g])

    def send(kind):
        exchange_own(kind).start()

        @pl.loop(1, 8)
        def _(d):
            exchange(kind, d).start()

    def send_global(e):
        @pl.loop(0, 4)
        def _(h):
            d = g ^ (4 * e + h)

            @pl.when(d == 0)
            def _():
                exchange_own(OG).start()

            @pl.when(d != 0)
            def _():
                exchange(OG, d).start()

    def sent(kind):
        @pl.loop(1, 8)
        def _(d):
            exchange(kind, d).wait_send()

    def received(kind):
        @pl.loop(0, 8)
        def _(t):
            _, dst = exchange_refs(kind, g)
            pltpu.make_async_copy(dst, dst, a2a_recv.at[kind, t]).wait()

    def hop(number, ref, device):
        return pltpu.make_async_remote_copy(
            src_ref=ref,
            dst_ref=ref,
            send_sem=ring_send.at[number],
            recv_sem=ring_recv.at[number],
            device_id=device,
            device_id_type=MESH,
        )

    def y_next(s):
        return line(z * NY + wrap(y + s, NY))

    def z_next(s):
        return line(wrap(z + s, NZ) * NY + y)

    def near(i):
        return wrap(z + (-((i + 1) // 2) if i % 2 else i // 2), NZ)

    def early_y(step, s):
        if step == 1:
            ref = kv.at[0, z, y]
        else:
            ref = kv.at[0, z, wrap(y - s, NY), 0 if s == 1 else 1]
        return hop(2 * (step - 1) + (s == 1), ref, y_next(s))

    def early_first(n, s):
        ref = kv.at[0, z, lax.rem(y + (0, 3, 1, 2)[n], NY)]
        return hop(18 + 2 * n + (s == 1), ref, z_next(s))

    def early_z(step, s):
        ref = kv.at[0, wrap(z - s * (step - 1), NZ)]
        if step == 4:
            ref = kv.at[0, wrap(z - s * (step - 1), NZ), :, 0 if s == 1 else 1]
        return hop(4 + 2 * (step - 2) + (s == 1), ref, z_next(s))

    def late_z(step, s):
        ref = kv.at[1, wrap(z - s * (step - 1), NZ), y]
        return hop(10 + 2 * (step - 1) + (s == 1), ref, z_next(s))

    def late_first(i, s):
        return hop(26 + 2 * i + (s == 1), kv.at[1, near(i), y], y_next(s))

    def late_second(i, s):
        ref = kv.at[1, near(i), wrap(y - s, NY), 0 if s == 1 else 1]
        return hop(42 + 2 * i + (s == 1), ref, y_next(s))

    def ways(family, step):
        return (-1,) if family in (late_z,) and step == 4 else (1, -1)

    def begin(family, *steps):
        for step in steps:
            for s in ways(family, step):
                family(step, s).start()

    def arrived(family, *steps):
        for step in steps:
            for s in ways(family, step):
                family(step, s).wait_recv()

    def left(family, *steps):
        for step in steps:
            for s in ways(family, step):
                family(step, s).wait_send()

    def halo_plane(e):
        return pltpu.make_async_remote_copy(
            src_ref=lkv.at[e, SPAN],
            dst_ref=lkv.at[jnp.where(z == NZ - 1, 1 - e, e), 0],
            send_sem=halo_send.at[e],
            recv_sem=halo_recv.at[jnp.where(z == NZ - 1, 1 - e, e)],
            device_id=z_next(1),
            device_id_type=MESH,
        )

    def halo_side(number, landing, source, target, s):
        return pltpu.make_async_remote_copy(
            src_ref=lkv.at[:, source],
            dst_ref=lkv.at[:, target],
            send_sem=halo_send.at[number],
            recv_sem=halo_recv.at[landing],
            device_id=y_next(s),
            device_id_type=MESH,
        )

    def halo_up():
        return halo_side(2, 2, jnp.where(y == NY - 1, 0, SPAN), SPAN - 1, 1)

    def halo_down():
        return halo_side(3, 3, jnp.where(y == 0, SPAN, 0), SPAN - 3, -1)

    def halo_on(s):
        return halo_side(4 + (s == 1), 4, SPAN - 1 if s == 1 else SPAN - 3, SPAN - 2, s)

    inner = (y == 1) | (y == 2)

    def halo_1():
        for e in range(2):
            halo_plane(e).start()
        pl.when(y != NY - 1)(lambda: halo_up().start())
        pl.when(y == 0)(lambda: halo_down().start())

    def halo_2():
        for e in range(2):
            halo_plane(e).wait_recv()
        pl.when(y == NY - 1)(lambda: halo_up().start())
        pl.when(y != 0)(lambda: halo_down().start())

    def halo_3():
        halo_up().wait_recv()
        halo_down().wait_recv()

        @pl.when(inner)
        def _():
            halo_on(1).start()
            halo_on(-1).start()

    def normalized(x):
        x = x.astype(jnp.float32)
        r = x * cos_ref[...] + pltpu.roll(x, HEAD // 2, 1) * sin_ref[...]
        mean = jnp.mean(r * r, axis=-1, keepdims=True)
        return (r * lax.rsqrt(mean + norm_epsilon)).astype(jnp.bfloat16)

    send(KG)
    send(VG)
    load_k.wait()
    for h in range(8):
        cols = slice(h * HEAD, (h + 1) * HEAD)
        nk[:, cols] = normalized(kl_ref[:, cols])
    load_q.wait()

    @pl.loop(0, 8)
    def _(t):
        for h in range(GROUP):
            cols = pl.ds(pl.multiple_of(t * WIDE + h * HEAD, HEAD), HEAD)
            nq[:, cols] = normalized(ql_ref[:, cols])

    m_ref[...] = jnp.full(m_ref.shape, masked_score, jnp.float32)
    acc[...] = jnp.zeros(acc.shape, jnp.float32)
    load_l.wait()

    @pl.loop(0, 2)
    def _(e):
        first = 8 * HEAD + (32 * e + c - SPAN) * TOK
        wide = jnp.concatenate(
            [labels[pl.ds(first // HEAD + n, 1), :] for n in range(9)], axis=1
        ).astype(jnp.float32)
        shifted = pltpu.roll(wide, 9 * HEAD - HEAD // 2, 1)
        wide = jnp.where(lax.rem(c, 2) == 1, shifted, wide)
        own = wide[:, SPAN * TOK : 8 * HEAD]
        row = lax.broadcasted_iota(jnp.int32, (TOK, 2 * HEAD), 0)
        col = lax.broadcasted_iota(jnp.int32, (TOK, 2 * HEAD), 1)
        mine = jnp.sum(jnp.where(row == col, own, 0.0), axis=1, keepdims=True)
        row_pos = lax.broadcasted_iota(jnp.int32, (TOK, KEYS), 0) + SPAN * TOK
        key_pos = lax.broadcasted_iota(jnp.int32, (TOK, KEYS), 1)
        allowed = (wide[:, :KEYS] == mine) & (key_pos <= row_pos)
        bias[e] = jnp.where(allowed, 0.0, masked_score)

    received(KG)
    received(VG)
    begin(late_z, 1)
    begin(early_y, 1)
    begin(early_first, 0)
    begin(late_first, 0)
    send(QG)
    arrived(early_y, 1)
    begin(early_y, 2)
    begin(early_first, 1, 2)
    arrived(late_z, 1)
    begin(late_z, 2)
    begin(late_first, 1, 2)
    arrived(early_y, 2)
    begin(early_first, 3)
    send(KL)
    send(VL)
    arrived(late_z, 2)
    begin(late_z, 3)
    begin(late_first, 3, 4)
    received(QG)

    @pl.loop(0, 2)
    def _(e):
        block = e * 32 + c
        pos = block * TOK + lax.broadcasted_iota(jnp.int32, (TOK, HEAD), 0)
        level = lax.shift_right_logical(pos + 1, temper_shift) + 1
        temper = 1.0 + temper_slope * jnp.log(level.astype(jnp.float32))
        factor = temper * (scaling * log2e)
        for h in range(GROUP):
            x = qg_buf[e, :, h * HEAD : (h + 1) * HEAD].astype(jnp.float32) * factor
            high = x.astype(jnp.bfloat16)
            low = (x - high.astype(jnp.float32)).astype(jnp.bfloat16)
            qs[e, h * TOK : (h + 1) * TOK, :] = jnp.concatenate([high, low], axis=1)

    def local_attention():
        received(QL)
        halo_on(1).wait_recv()

        @pl.loop(0, 2)
        def _(e):
            k = lkv[e, :, 0].reshape(KEYS, HEAD)
            v = lkv[e, :, 1].reshape(KEYS, HEAD)
            va = jnp.concatenate([v, jnp.ones((KEYS, HEAD), jnp.bfloat16)], axis=1)
            for h in range(GROUP):
                cols = slice(h * HEAD, (h + 1) * HEAD)
                s = lax.dot_general(
                    lq_buf[e, :, cols], k, (((1,), (1,)), ((), ())),
                    preferred_element_type=jnp.float32,
                )
                p = jnp.exp2(s * (scaling * log2e) + bias[e]).astype(jnp.bfloat16)
                o = jnp.dot(p, va, preferred_element_type=jnp.float32)
                ol_buf[e, :, cols] = (o[:, :HEAD] / o[:, HEAD:]).astype(jnp.bfloat16)

        send(OL)

    def unit(eq, ek, zs, ys, start=None, slope=None):
        k = jnp.concatenate([kv[ek, zs[n], ys[n], 0] for n in range(4)], axis=0)
        v = jnp.concatenate([kv[ek, zs[n], ys[n], 1] for n in range(4)], axis=0)
        kk = jnp.concatenate([k, k], axis=1)
        va = jnp.concatenate([v, jnp.ones((CHUNK, HEAD), jnp.bfloat16)], axis=1)
        for t in range(ROWS // TILE):
            rows = pl.ds(t * TILE, TILE)
            s = lax.dot_general(
                qs[eq, rows, :], kk, (((1,), (1,)), ((), ())),
                preferred_element_type=jnp.float32,
            )
            if start is not None:
                r = t * TILE + lax.broadcasted_iota(jnp.int32, (TILE, HEAD), 0)
                for h in range(GROUP - 1, 0, -1):
                    r = jnp.where(r >= h * TOK, r - h * TOK, r)
                limit = tiled(r * slope + start, CHUNK // HEAD)
                key = lax.broadcasted_iota(jnp.int32, (TILE, CHUNK), 1)
                s = jnp.where(key <= limit, s, masked_score)
            before = m_ref[eq, rows, :]
            peak = jnp.maximum(before, jnp.max(s, axis=1, keepdims=True))
            factor = jnp.exp2(before - peak)
            p = jnp.exp2(s - tiled(peak, CHUNK // HEAD)).astype(jnp.bfloat16)
            acc[eq, rows, :] = acc[eq, rows, :] * tiled(factor, 2) + jnp.dot(
                p, va, preferred_element_type=jnp.float32
            )
            m_ref[eq, rows, :] = peak

    def finish(e):
        for h in range(GROUP):
            o = acc[e, h * TOK : (h + 1) * TOK, :]
            og_buf[e, :, h * HEAD : (h + 1) * HEAD] = (o[:, :HEAD] / o[:, HEAD:]).astype(
                jnp.bfloat16
            )
        send_global(e)

    def service_1():
        arrived(late_z, 3)
        begin(late_z, 4)
        begin(late_first, 5, 6)
        arrived(early_first, 0, 1, 2, 3)
        begin(early_z, 2)
        received(KL)
        received(VL)
        halo_1()
        send(QL)

    def service_2():
        arrived(late_z, 4)
        begin(late_first, 7)
        halo_2()

    def service_3():
        for i in range(5):
            arrived(late_first, i)
            begin(late_second, i)

    def service_4():
        arrived(early_z, 2)
        begin(early_z, 3)
        for i in range(5, 8):
            arrived(late_first, i)
            begin(late_second, i)
        halo_3()

    def service_8():
        arrived(early_z, 3)
        begin(early_z, 4)
        local_attention()

    def service_10():
        arrived(early_z, 4)

    def service_11():
        finish(0)
        arrived(late_second, *range(8))

    services = {
        1: service_1,
        2: service_2,
        3: service_3,
        4: service_4,
        8: service_8,
        10: service_10,
        11: service_11,
    }

    @pl.loop(0, 24)
    def _(j):
        pair = j // 2
        second = lax.rem(j, 2)
        for at_pair, action in services.items():
            pl.when(j == 2 * at_pair)(action)

        column = (pair == 3) | (pair == 6) | (pair == 7) | (pair == 11)
        i = jnp.where(pair < 3, pair, jnp.where(pair < 6, pair - 1, pair - 3))
        away = (i + 1) // 2
        chunk = lax.rem(z + jnp.where(lax.rem(i, 2) == 1, 8 - away, away), NZ)
        turn = jnp.where(pair == 3, 0, jnp.where(pair == 6, 3, jnp.where(pair == 7, 1, 2)))
        y_col = lax.rem(y + turn, NY)
        z_rel = z - 4 * second

        early_query = jnp.logical_not(column) & (second == 1)
        eq = jnp.where(early_query, 0, 1)
        ek = jnp.where(column, 1, 0)
        do = jnp.where(column, z_rel >= 0, (second == 0) | (chunk <= z))
        masked = jnp.where(column, z_rel <= 3, (second == 1) & (chunk == z))
        slope = jnp.where(column & (y_col != y), 0, 1)
        start = jnp.where(
            column,
            z_rel * TOK + jnp.where(y_col < y, TOK - 1, jnp.where(y_col == y, 0, -1)),
            y * TOK,
        )
        zs = [jnp.where(column, 4 * second + n, chunk) for n in range(4)]
        ys = [jnp.where(column, y_col, n) for n in range(4)]

        @pl.when(do & jnp.logical_not(masked))
        def _():
            unit(eq, ek, zs, ys)

        @pl.when(do & masked)
        def _():
            unit(eq, ek, zs, ys, start, slope)

    finish(1)
    for kind in (KG, VG, KL, VL, QL, QG, OL):
        sent(kind)
    left(early_y, 1, 2)
    left(early_first, 0, 1, 2, 3)
    left(early_z, 2, 3, 4)
    left(late_z, 1, 2, 3, 4)
    left(late_first, *range(8))
    left(late_second, *range(8))
    for e in range(2):
        halo_plane(e).wait_send()
    halo_up().wait_send()
    halo_down().wait_send()

    @pl.when(inner)
    def _():
        halo_on(1).wait_send()
        halo_on(-1).wait_send()

    received(OL)
    received(OG)
    sent(OG)


def shards(
    query_local, key_local, value_local, stretch_labels, query_global, key_global, value_global
):
    ctx = lax.axis_index("ctx")
    head = lax.axis_index("head")
    positions = (ctx * TOK + head * OWN + jnp.arange(OWN, dtype=jnp.int32)).astype(jnp.float32)
    half = HEAD // 2
    frequency = rope_base ** (-(jnp.arange(half, dtype=jnp.float32) * 2.0 / HEAD))
    angles = positions[:, None] * frequency[None, :]
    cosine, sine = jnp.cos(angles), jnp.sin(angles)
    cosine = jnp.concatenate([cosine, cosine], axis=1)
    sine = jnp.concatenate([-sine, sine], axis=1)
    any_space = pl.BlockSpec(memory_space=pl.ANY)
    vmem = pl.BlockSpec(memory_space=pltpu.VMEM)
    bf16, f32 = jnp.bfloat16, jnp.float32
    out = jax.ShapeDtypeStruct(query_local.shape, bf16)
    return pl.pallas_call(
        kernel,
        out_shape=(out, out),
        in_specs=[any_space] * 6 + [vmem] * 2 + [any_space],
        out_specs=(any_space, any_space),
        scratch_shapes=[
            pltpu.VMEM((OWN, 8 * WIDE), bf16),
            pltpu.VMEM((OWN, 8 * HEAD), bf16),
            pltpu.VMEM((112, HEAD), jnp.int32),
            pltpu.VMEM((2, NZ, NY, 2, TOK, HEAD), bf16),
            pltpu.VMEM((2, SPAN + 1, 2, TOK, HEAD), bf16),
            pltpu.VMEM((2, TOK, WIDE), bf16),
            pltpu.VMEM((2, TOK, WIDE), bf16),
            pltpu.VMEM((OWN, 8 * WIDE), bf16),
            pltpu.VMEM((OWN, 8 * HEAD), bf16),
            pltpu.VMEM((2, ROWS, 2 * HEAD), bf16),
            pltpu.VMEM((2, ROWS, HEAD), f32),
            pltpu.VMEM((2, ROWS, 2 * HEAD), f32),
            pltpu.VMEM((2, TOK, WIDE), bf16),
            pltpu.VMEM((2, TOK, WIDE), bf16),
            pltpu.VMEM((2, TOK, KEYS), f32),
            pltpu.SemaphoreType.DMA((8, 8)),
            pltpu.SemaphoreType.DMA((8, 8)),
            pltpu.SemaphoreType.DMA((58,)),
            pltpu.SemaphoreType.DMA((58,)),
            pltpu.SemaphoreType.DMA((6,)),
            pltpu.SemaphoreType.DMA((5,)),
            pltpu.SemaphoreType.DMA((3,)),
        ],
        compiler_params=pltpu.CompilerParams(
            collective_id=0, has_side_effects=True, vmem_limit_bytes=62 << 20
        ),
    )(
        query_local, key_local, value_local, query_global, key_global, value_global,
        cosine, sine, stretch_labels.reshape(-1, HEAD),
    )


def solution(mesh):
    rows = P(("ctx", "head"), None)
    return jax.shard_map(
        shards,
        mesh=mesh,
        in_specs=(rows, rows, rows, P(), rows, rows, rows),
        out_specs=(rows, rows),
        check_vma=False,
    )
```

```python
import functools

import jax
import jax.numpy as jnp
from jax import lax
from jax.experimental import pallas as pl
from jax.experimental.pallas import tpu as pltpu
from jax.sharding import PartitionSpec as P

HEAD = 128
GROUP = 5
WIDE = GROUP * HEAD
TOK = 192
OWN = 48
NZ, NY = 8, 4
ROWS = GROUP * TOK
CHUNK = NY * TOK
SPAN = 4
KEYS = (SPAN + 1) * TOK
TILE = 320

rope_base = 500000.0
norm_epsilon = 1e-06
temper_shift = 13
temper_slope = 0.1
masked_score = -1e30
log2e = 1.4426950408889634
scaling = HEAD ** (-0.5)

MESH = pl.DeviceIdType.MESH
KG, VG, KL, VL, QL, QG, OL, OG = range(8)


def tiled(x, n):
    return jnp.concatenate([x] * n, axis=1)


def kernel(
    ql_hbm, kl_hbm, vl_hbm, qg_hbm, kg_hbm, vg_hbm, cos_ref, sin_ref, label_hbm,
    ol_hbm, og_hbm,
    ql_ref, kl_ref, labels, kv, lkv, qg_buf, lq_buf, nq, nk, qs, m_ref, acc, og_buf, ol_buf, bias,
    a2a_send, a2a_recv, ring_send, ring_recv, halo_send, halo_recv, load_sem,
):
    ctx = lax.axis_index("ctx")
    head = lax.axis_index("head")
    x_lo = ctx // 32
    c = ctx % 32
    z = c // NY
    y = c % NY
    g = x_lo * 4 + head

    def at(row, member):
        return {"ctx": (member // 4) * 32 + row, "head": member % 4}

    def line(row):
        return {"ctx": x_lo * 32 + row, "head": head}

    def wrap(v, n):
        return lax.rem(v + n, n)

    barrier = pltpu.get_barrier_semaphore()

    def greet(device):
        pl.semaphore_signal(barrier, inc=1, device_id=device, device_id_type=MESH)

    @pl.loop(1, 8)
    def _(t):
        greet(at(c, g ^ t))

    for s in (1, -1):
        greet(line(z * NY + wrap(y + s, NY)))
        greet(line(wrap(z + s, NZ) * NY + y))

    load_k = pltpu.make_async_copy(kl_hbm, kl_ref, load_sem.at[0])
    load_q = pltpu.make_async_copy(ql_hbm, ql_ref, load_sem.at[1])
    labels[:8, :] = jnp.full((8, HEAD), -1, jnp.int32)
    labels[104:, :] = jnp.full((8, HEAD), -1, jnp.int32)
    load_l = pltpu.make_async_copy(label_hbm, labels.at[8:104, :], load_sem.at[2])
    load_l.start()
    load_k.start()
    load_q.start()
    pl.semaphore_wait(barrier, 11)

    my_rows = pl.ds(head * OWN, OWN)

    def exchange_refs(kind, target):
        narrow = pl.ds(pl.multiple_of(target * HEAD, HEAD), HEAD)
        wide = pl.ds(pl.multiple_of(target * WIDE, HEAD), WIDE)
        mine = pl.ds(pl.multiple_of(g * WIDE, HEAD), WIDE)
        their = pl.ds(lax.rem(target, 4) * OWN, OWN)
        if kind == KG:
            return kg_hbm.at[:, narrow], kv.at[x_lo, z, y, 0, my_rows, :]
        if kind == VG:
            return vg_hbm.at[:, narrow], kv.at[x_lo, z, y, 1, my_rows, :]
        if kind == KL:
            return nk.at[:, narrow], lkv.at[x_lo, SPAN, 0, my_rows, :]
        if kind == VL:
            return vl_hbm.at[:, narrow], lkv.at[x_lo, SPAN, 1, my_rows, :]
        if kind == QL:
            return nq.at[:, wide], lq_buf.at[x_lo, my_rows, :]
        if kind == QG:
            return qg_hbm.at[:, wide], qg_buf.at[x_lo, my_rows, :]
        if kind == OL:
            return ol_buf.at[target // 4, their, :], ol_hbm.at[:, mine]
        return og_buf.at[target // 4, their, :], og_hbm.at[:, mine]

    def exchange(kind, d):
        target = g ^ d
        src, dst = exchange_refs(kind, target)
        return pltpu.make_async_remote_copy(
            src_ref=src,
            dst_ref=dst,
            send_sem=a2a_send.at[kind, d],
            recv_sem=a2a_recv.at[kind, g],
            device_id=at(c, target),
            device_id_type=MESH,
        )

    def exchange_own(kind):
        src, dst = exchange_refs(kind, g)
        return pltpu.make_async_copy(src, dst, a2a_recv.at[kind, g])

    def send(kind):
        exchange_own(kind).start()

        @pl.loop(1, 8)
        def _(d):
            exchange(kind, d).start()

    def send_global(e):
        @pl.loop(0, 4)
        def _(h):
            d = g ^ (4 * e + h)

            @pl.when(d == 0)
            def _():
                exchange_own(OG).start()

            @pl.when(d != 0)
            def _():
                exchange(OG, d).start()

    def sent(kind):
        @pl.loop(1, 8)
        def _(d):
            exchange(kind, d).wait_send()

    def received(kind):
        @pl.loop(0, 8)
        def _(t):
            _, dst = exchange_refs(kind, g)
            pltpu.make_async_copy(dst, dst, a2a_recv.at[kind, t]).wait()

    def hop(number, ref, device):
        return pltpu.make_async_remote_copy(
            src_ref=ref,
            dst_ref=ref,
            send_sem=ring_send.at[number],
            recv_sem=ring_recv.at[number],
            device_id=device,
            device_id_type=MESH,
        )

    def y_next(s):
        return line(z * NY + wrap(y + s, NY))

    def z_next(s):
        return line(wrap(z + s, NZ) * NY + y)

    def near(i):
        return wrap(z + (-((i + 1) // 2) if i % 2 else i // 2), NZ)

    def early_y(step, s):
        if step == 1:
            ref = kv.at[0, z, y]
        else:
            ref = kv.at[0, z, wrap(y - s, NY), 0 if s == 1 else 1]
        return hop(2 * (step - 1) + (s == 1), ref, y_next(s))

    def early_first(n, s):
        ref = kv.at[0, z, lax.rem(y + (0, 3, 1, 2)[n], NY)]
        return hop(18 + 2 * n + (s == 1), ref, z_next(s))

    def early_z(step, s):
        ref = kv.at[0, wrap(z - s * (step - 1), NZ)]
        if step == 4:
            ref = kv.at[0, wrap(z - s * (step - 1), NZ), :, 0 if s == 1 else 1]
        return hop(4 + 2 * (step - 2) + (s == 1), ref, z_next(s))

    def late_z(step, s):
        ref = kv.at[1, wrap(z - s * (step - 1), NZ), y]
        return hop(10 + 2 * (step - 1) + (s == 1), ref, z_next(s))

    def late_first(i, s):
        return hop(26 + 2 * i + (s == 1), kv.at[1, near(i), y], y_next(s))

    def late_second(i, s):
        ref = kv.at[1, near(i), wrap(y - s, NY), 0 if s == 1 else 1]
        return hop(42 + 2 * i + (s == 1), ref, y_next(s))

    def ways(family, step):
        return (-1,) if family in (late_z,) and step == 4 else (1, -1)

    def begin(family, *steps):
        for step in steps:
            for s in ways(family, step):
                family(step, s).start()

    def arrived(family, *steps):
        for step in steps:
            for s in ways(family, step):
                family(step, s).wait_recv()

    def left(family, *steps):
        for step in steps:
            for s in ways(family, step):
                family(step, s).wait_send()

    def halo_plane(e):
        return pltpu.make_async_remote_copy(
            src_ref=lkv.at[e, SPAN],
            dst_ref=lkv.at[jnp.where(z == NZ - 1, 1 - e, e), 0],
            send_sem=halo_send.at[e],
            recv_sem=halo_recv.at[jnp.where(z == NZ - 1, 1 - e, e)],
            device_id=z_next(1),
            device_id_type=MESH,
        )

    def halo_side(number, landing, source, target, s):
        return pltpu.make_async_remote_copy(
            src_ref=lkv.at[:, source],
            dst_ref=lkv.at[:, target],
            send_sem=halo_send.at[number],
            recv_sem=halo_recv.at[landing],
            device_id=y_next(s),
            device_id_type=MESH,
        )

    def halo_up():
        return halo_side(2, 2, jnp.where(y == NY - 1, 0, SPAN), SPAN - 1, 1)

    def halo_down():
        return halo_side(3, 3, jnp.where(y == 0, SPAN, 0), SPAN - 3, -1)

    def halo_on(s):
        return halo_side(4 + (s == 1), 4, SPAN - 1 if s == 1 else SPAN - 3, SPAN - 2, s)

    inner = (y == 1) | (y == 2)

    def halo_1():
        for e in range(2):
            halo_plane(e).start()
        pl.when(y != NY - 1)(lambda: halo_up().start())
        pl.when(y == 0)(lambda: halo_down().start())

    def halo_2():
        for e in range(2):
            halo_plane(e).wait_recv()
        pl.when(y == NY - 1)(lambda: halo_up().start())
        pl.when(y != 0)(lambda: halo_down().start())

    def halo_3():
        halo_up().wait_recv()
        halo_down().wait_recv()

        @pl.when(inner)
        def _():
            halo_on(1).start()
            halo_on(-1).start()

    def normalized(x):
        x = x.astype(jnp.float32)
        r = x * cos_ref[...] + pltpu.roll(x, HEAD // 2, 1) * sin_ref[...]
        mean = jnp.mean(r * r, axis=-1, keepdims=True)
        return (r * lax.rsqrt(mean + norm_epsilon)).astype(jnp.bfloat16)

    send(KG)
    send(VG)
    load_k.wait()
    for h in range(8):
        cols = slice(h * HEAD, (h + 1) * HEAD)
        nk[:, cols] = normalized(kl_ref[:, cols])
    load_q.wait()

    @pl.loop(0, 8)
    def _(t):
        for h in range(GROUP):
            cols = pl.ds(pl.multiple_of(t * WIDE + h * HEAD, HEAD), HEAD)
            nq[:, cols] = normalized(ql_ref[:, cols])

    m_ref[...] = jnp.full(m_ref.shape, masked_score, jnp.float32)
    acc[...] = jnp.zeros(acc.shape, jnp.float32)
    load_l.wait()

    @pl.loop(0, 2)
    def _(e):
        first = 8 * HEAD + (32 * e + c - SPAN) * TOK
        wide = jnp.concatenate(
            [labels[pl.ds(first // HEAD + n, 1), :] for n in range(9)], axis=1
        ).astype(jnp.float32)
        shifted = pltpu.roll(wide, 9 * HEAD - HEAD // 2, 1)
        wide = jnp.where(lax.rem(c, 2) == 1, shifted, wide)
        own = wide[:, SPAN * TOK : 8 * HEAD]
        row = lax.broadcasted_iota(jnp.int32, (TOK, 2 * HEAD), 0)
        col = lax.broadcasted_iota(jnp.int32, (TOK, 2 * HEAD), 1)
        mine = jnp.sum(jnp.where(row == col, own, 0.0), axis=1, keepdims=True)
        row_pos = lax.broadcasted_iota(jnp.int32, (TOK, KEYS), 0) + SPAN * TOK
        key_pos = lax.broadcasted_iota(jnp.int32, (TOK, KEYS), 1)
        allowed = (wide[:, :KEYS] == mine) & (key_pos <= row_pos)
        bias[e] = jnp.where(allowed, 0.0, masked_score)

    received(KG)
    received(VG)
    begin(late_z, 1)
    begin(early_y, 1)
    begin(early_first, 0)
    begin(late_first, 0)
    send(QG)
    arrived(early_y, 1)
    begin(early_y, 2)
    begin(early_first, 1, 2)
    arrived(late_z, 1)
    begin(late_z, 2)
    begin(late_first, 1, 2)
    arrived(early_y, 2)
    begin(early_first, 3)
    send(KL)
    send(VL)
    arrived(late_z, 2)
    begin(late_z, 3)
    begin(late_first, 3, 4)
    received(QG)

    @pl.loop(0, 2)
    def _(e):
        block = e * 32 + c
        pos = block * TOK + lax.broadcasted_iota(jnp.int32, (TOK, HEAD), 0)
        level = lax.shift_right_logical(pos + 1, temper_shift) + 1
        temper = 1.0 + temper_slope * jnp.log(level.astype(jnp.float32))
        factor = temper * (scaling * log2e)
        for h in range(GROUP):
            x = qg_buf[e, :, h * HEAD : (h + 1) * HEAD].astype(jnp.float32) * factor
            high = x.astype(jnp.bfloat16)
            low = (x - high.astype(jnp.float32)).astype(jnp.bfloat16)
            qs[e, h * TOK : (h + 1) * TOK, :] = jnp.concatenate([high, low], axis=1)

    def local_attention():
        received(QL)
        halo_on(1).wait_recv()

        @pl.loop(0, 2)
        def _(e):
            k = lkv[e, :, 0].reshape(KEYS, HEAD)
            v = lkv[e, :, 1].reshape(KEYS, HEAD)
            va = jnp.concatenate([v, jnp.ones((KEYS, HEAD), jnp.bfloat16)], axis=1)
            for h in range(GROUP):
                cols = slice(h * HEAD, (h + 1) * HEAD)
                s = lax.dot_general(
                    lq_buf[e, :, cols], k, (((1,), (1,)), ((), ())),
                    preferred_element_type=jnp.float32,
                )
                p = jnp.exp2(s * (scaling * log2e) + bias[e]).astype(jnp.bfloat16)
                o = jnp.dot(p, va, preferred_element_type=jnp.float32)
                ol_buf[e, :, cols] = (o[:, :HEAD] / o[:, HEAD:]).astype(jnp.bfloat16)

        send(OL)

    def unit(eq, ek, zs, ys, start=None, slope=None):
        keys = TOK * len(zs)
        k = jnp.concatenate([kv[ek, a, b, 0] for a, b in zip(zs, ys)], axis=0)
        v = jnp.concatenate([kv[ek, a, b, 1] for a, b in zip(zs, ys)], axis=0)
        kk = jnp.concatenate([k, k], axis=1)
        va = jnp.concatenate([v, jnp.ones((keys, HEAD), jnp.bfloat16)], axis=1)

        def scores(t):
            return lax.dot_general(
                qs[eq, t * TILE : (t + 1) * TILE, :], kk, (((1,), (1,)), ((), ())),
                preferred_element_type=jnp.float32,
            )

        ahead = scores(0)
        for t in range(ROWS // TILE):
            rows = pl.ds(t * TILE, TILE)
            s = ahead
            if t + 1 < ROWS // TILE:
                ahead = scores(t + 1)
            if start is not None:
                r = t * TILE + lax.broadcasted_iota(jnp.int32, (TILE, HEAD), 0)
                for h in range(GROUP - 1, 0, -1):
                    r = jnp.where(r >= h * TOK, r - h * TOK, r)
                limit = tiled(r * slope + (start - (keys - CHUNK)), CHUNK // HEAD)
                key = lax.broadcasted_iota(jnp.int32, (TILE, CHUNK), 1)
                last = jnp.where(key <= limit, s[:, keys - CHUNK :], masked_score)
                s = last if keys == CHUNK else jnp.concatenate([s[:, : keys - CHUNK], last], 1)
            before = m_ref[eq, rows, :]
            peak = jnp.maximum(before, jnp.max(s, axis=1, keepdims=True))
            factor = jnp.exp2(before - peak)
            p = jnp.exp2(s - tiled(peak, keys // HEAD)).astype(jnp.bfloat16)
            acc[eq, rows, :] = acc[eq, rows, :] * tiled(factor, 2) + jnp.dot(
                p, va, preferred_element_type=jnp.float32
            )
            m_ref[eq, rows, :] = peak

    def finish(e):
        for h in range(GROUP):
            o = acc[e, h * TOK : (h + 1) * TOK, :]
            og_buf[e, :, h * HEAD : (h + 1) * HEAD] = (o[:, :HEAD] / o[:, HEAD:]).astype(
                jnp.bfloat16
            )
        send_global(e)

    def service_1():
        arrived(late_z, 3)
        begin(late_z, 4)
        begin(late_first, 5, 6)
        arrived(early_first, 0, 1, 2, 3)
        begin(early_z, 2)
        received(KL)
        received(VL)
        halo_1()
        send(QL)

    def service_2():
        arrived(late_z, 4)
        begin(late_first, 7)
        halo_2()

    def service_3():
        for i in range(5):
            arrived(late_first, i)
            begin(late_second, i)

    def service_4():
        arrived(early_z, 2)
        begin(early_z, 3)
        for i in range(5, 8):
            arrived(late_first, i)
            begin(late_second, i)
        halo_3()

    def service_8():
        arrived(early_z, 3)
        begin(early_z, 4)
        local_attention()

    def service_10():
        arrived(early_z, 4)

    def service_11():
        finish(0)
        arrived(late_second, *range(8))

    services = {
        2: service_1,
        3: service_2,
        4: service_3,
        6: service_4,
        12: service_8,
        14: service_10,
        16: service_11,
    }

    @pl.loop(0, 17)
    def _(j):
        slot = j // 2
        second = lax.rem(j, 2) == 1
        for place, action in services.items():
            pl.when(j == place)(action)

        column = (slot == 2) | (slot == 4) | (slot == 5) | (slot == 8)
        far = jnp.where(slot < 2, slot, jnp.where(slot == 3, 2, slot - 3))
        below = lax.rem(z - far + NZ, NZ)
        above = lax.rem(z + far, NZ)
        turn = jnp.where(slot == 2, 0, jnp.where(slot == 4, 3, jnp.where(slot == 5, 1, 2)))
        y_col = lax.rem(y + turn, NY)

        two = (far > 0) & (far < 4)
        wide = jnp.where(column, z >= 4, two & (jnp.logical_not(second) | (z + far >= NZ)))
        do = jnp.where(column, jnp.logical_not(second), jnp.logical_not(second) | (z >= far))
        masked = column | (second & (far == 0))
        eq = jnp.where(jnp.logical_not(column) & second, 0, 1)
        ek = jnp.where(column, 1, 0)
        slope = jnp.where(column & (y_col != y), 0, 1)
        start = jnp.where(
            column,
            z * TOK + jnp.where(y_col < y, TOK - 1, jnp.where(y_col == y, 0, -1)),
            y * TOK,
        )
        zs = [jnp.where(column, n, below if n < 4 else above) for n in range(8)]
        ys = [jnp.where(column, y_col, n % 4) for n in range(8)]
        free = jnp.logical_not(masked)
        narrow = jnp.logical_not(wide)

        @pl.when(do & narrow & free)
        def _():
            unit(eq, ek, zs[:4], ys[:4])

        @pl.when(do & narrow & masked)
        def _():
            unit(eq, ek, zs[:4], ys[:4], start, slope)

        @pl.when(do & wide & free)
        def _():
            unit(eq, ek, zs, ys)

        @pl.when(do & wide & masked)
        def _():
            unit(eq, ek, zs, ys, start, slope)

    finish(1)
    for kind in (KG, VG, KL, VL, QL, QG, OL):
        sent(kind)
    left(early_y, 1, 2)
    left(early_first, 0, 1, 2, 3)
    left(early_z, 2, 3, 4)
    left(late_z, 1, 2, 3, 4)
    left(late_first, *range(8))
    left(late_second, *range(8))
    for e in range(2):
        halo_plane(e).wait_send()
    halo_up().wait_send()
    halo_down().wait_send()

    @pl.when(inner)
    def _():
        halo_on(1).wait_send()
        halo_on(-1).wait_send()

    received(OL)
    received(OG)
    sent(OG)


def shards(
    query_local, key_local, value_local, stretch_labels, query_global, key_global, value_global
):
    ctx = lax.axis_index("ctx")
    head = lax.axis_index("head")
    positions = (ctx * TOK + head * OWN + jnp.arange(OWN, dtype=jnp.int32)).astype(jnp.float32)
    half = HEAD // 2
    frequency = rope_base ** (-(jnp.arange(half, dtype=jnp.float32) * 2.0 / HEAD))
    angles = positions[:, None] * frequency[None, :]
    cosine, sine = jnp.cos(angles), jnp.sin(angles)
    cosine = jnp.concatenate([cosine, cosine], axis=1)
    sine = jnp.concatenate([-sine, sine], axis=1)
    any_space = pl.BlockSpec(memory_space=pl.ANY)
    vmem = pl.BlockSpec(memory_space=pltpu.VMEM)
    bf16, f32 = jnp.bfloat16, jnp.float32
    out = jax.ShapeDtypeStruct(query_local.shape, bf16)
    return pl.pallas_call(
        kernel,
        out_shape=(out, out),
        in_specs=[any_space] * 6 + [vmem] * 2 + [any_space],
        out_specs=(any_space, any_space),
        scratch_shapes=[
            pltpu.VMEM((OWN, 8 * WIDE), bf16),
            pltpu.VMEM((OWN, 8 * HEAD), bf16),
            pltpu.VMEM((112, HEAD), jnp.int32),
            pltpu.VMEM((2, NZ, NY, 2, TOK, HEAD), bf16),
            pltpu.VMEM((2, SPAN + 1, 2, TOK, HEAD), bf16),
            pltpu.VMEM((2, TOK, WIDE), bf16),
            pltpu.VMEM((2, TOK, WIDE), bf16),
            pltpu.VMEM((OWN, 8 * WIDE), bf16),
            pltpu.VMEM((OWN, 8 * HEAD), bf16),
            pltpu.VMEM((2, ROWS, 2 * HEAD), bf16),
            pltpu.VMEM((2, ROWS, HEAD), f32),
            pltpu.VMEM((2, ROWS, 2 * HEAD), f32),
            pltpu.VMEM((2, TOK, WIDE), bf16),
            pltpu.VMEM((2, TOK, WIDE), bf16),
            pltpu.VMEM((2, TOK, KEYS), f32),
            pltpu.SemaphoreType.DMA((8, 8)),
            pltpu.SemaphoreType.DMA((8, 8)),
            pltpu.SemaphoreType.DMA((58,)),
            pltpu.SemaphoreType.DMA((58,)),
            pltpu.SemaphoreType.DMA((6,)),
            pltpu.SemaphoreType.DMA((5,)),
            pltpu.SemaphoreType.DMA((3,)),
        ],
        compiler_params=pltpu.CompilerParams(
            collective_id=0, has_side_effects=True, vmem_limit_bytes=62 << 20
        ),
    )(
        query_local, key_local, value_local, query_global, key_global, value_global,
        cosine, sine, stretch_labels.reshape(-1, HEAD),
    )


def solution(mesh):
    rows = P(("ctx", "head"), None)
    return jax.shard_map(
        shards,
        mesh=mesh,
        in_specs=(rows, rows, rows, P(), rows, rows, rows),
        out_specs=(rows, rows),
        check_vma=False,
    )
```

```python
import functools

import jax
import jax.numpy as jnp
from jax import lax
from jax.experimental import pallas as pl
from jax.experimental.pallas import tpu as pltpu
from jax.sharding import PartitionSpec as P

HEAD = 128
GROUP = 5
WIDE = GROUP * HEAD
TOK = 192
OWN = 48
NZ, NY = 8, 4
ROWS = GROUP * TOK
CHUNK = NY * TOK
SPAN = 4
KEYS = (SPAN + 1) * TOK
TILE = 320

rope_base = 500000.0
norm_epsilon = 1e-06
temper_shift = 13
temper_slope = 0.1
masked_score = -1e30
log2e = 1.4426950408889634
scaling = HEAD ** (-0.5)

MESH = pl.DeviceIdType.MESH
KG, VG, KL, VL, QL, QG, OL, OG = range(8)


def tiled(x, n):
    return jnp.concatenate([x] * n, axis=1)


def kernel(
    ql_hbm, kl_hbm, vl_hbm, qg_hbm, kg_hbm, vg_hbm, cos_hbm, sin_hbm, label_hbm,
    ol_hbm, og_hbm,
    ql_ref, kl_ref, cos_half, sin_half, cos_ref, sin_ref, labels, kv, lkv, qg_buf, lq_buf, nq, nk, qs, m_ref, acc, og_buf, ol_buf, bias,
    a2a_send, a2a_recv, ring_send, ring_recv, halo_send, halo_recv, load_sem,
):
    ctx = lax.axis_index("ctx")
    head = lax.axis_index("head")
    x_lo = ctx // 32
    c = ctx % 32
    z = c // NY
    y = c % NY
    g = x_lo * 4 + head

    def at(row, member):
        return {"ctx": (member // 4) * 32 + row, "head": member % 4}

    def line(row):
        return {"ctx": x_lo * 32 + row, "head": head}

    def wrap(v, n):
        return lax.rem(v + n, n)

    barrier = pltpu.get_barrier_semaphore()

    def greet(device):
        pl.semaphore_signal(barrier, inc=1, device_id=device, device_id_type=MESH)

    @pl.loop(1, 8)
    def _(t):
        greet(at(c, g ^ t))

    for s in (1, -1):
        greet(line(z * NY + wrap(y + s, NY)))
        greet(line(wrap(z + s, NZ) * NY + y))

    load_k = pltpu.make_async_copy(kl_hbm, kl_ref, load_sem.at[0])
    load_q = pltpu.make_async_copy(ql_hbm, ql_ref, load_sem.at[1])
    labels[:8, :] = jnp.full((8, HEAD), -1, jnp.int32)
    labels[104:, :] = jnp.full((8, HEAD), -1, jnp.int32)
    load_l = pltpu.make_async_copy(label_hbm, labels.at[8:104, :], load_sem.at[2])
    load_l.start()
    load_c = pltpu.make_async_copy(cos_hbm, cos_half, load_sem.at[3])
    load_s = pltpu.make_async_copy(sin_hbm, sin_half, load_sem.at[4])
    load_c.start()
    load_s.start()
    load_k.start()
    load_q.start()
    pl.semaphore_wait(barrier, 11)

    my_rows = pl.ds(head * OWN, OWN)

    def exchange_refs(kind, target):
        narrow = pl.ds(pl.multiple_of(target * HEAD, HEAD), HEAD)
        wide = pl.ds(pl.multiple_of(target * WIDE, HEAD), WIDE)
        mine = pl.ds(pl.multiple_of(g * WIDE, HEAD), WIDE)
        their = pl.ds(lax.rem(target, 4) * OWN, OWN)
        if kind == KG:
            return kg_hbm.at[:, narrow], kv.at[x_lo, z, y, 0, my_rows, :]
        if kind == VG:
            return vg_hbm.at[:, narrow], kv.at[x_lo, z, y, 1, my_rows, :]
        if kind == KL:
            return nk.at[:, narrow], lkv.at[x_lo, SPAN, 0, my_rows, :]
        if kind == VL:
            return vl_hbm.at[:, narrow], lkv.at[x_lo, SPAN, 1, my_rows, :]
        if kind == QL:
            return nq.at[:, wide], lq_buf.at[x_lo, my_rows, :]
        if kind == QG:
            return qg_hbm.at[:, wide], qg_buf.at[x_lo, my_rows, :]
        if kind == OL:
            return ol_buf.at[target // 4, their, :], ol_hbm.at[:, mine]
        return og_buf.at[target // 4, their, :], og_hbm.at[:, mine]

    def exchange(kind, d):
        target = g ^ d
        src, dst = exchange_refs(kind, target)
        return pltpu.make_async_remote_copy(
            src_ref=src,
            dst_ref=dst,
            send_sem=a2a_send.at[kind, d],
            recv_sem=a2a_recv.at[kind, g],
            device_id=at(c, target),
            device_id_type=MESH,
        )

    def exchange_own(kind):
        src, dst = exchange_refs(kind, g)
        return pltpu.make_async_copy(src, dst, a2a_recv.at[kind, g])

    def send(kind):
        exchange_own(kind).start()

        @pl.loop(1, 8)
        def _(d):
            exchange(kind, d).start()

    def send_global(e):
        @pl.loop(0, 4)
        def _(h):
            d = g ^ (4 * e + h)

            @pl.when(d == 0)
            def _():
                exchange_own(OG).start()

            @pl.when(d != 0)
            def _():
                exchange(OG, d).start()

    def sent(kind):
        @pl.loop(1, 8)
        def _(d):
            exchange(kind, d).wait_send()

    def received(kind):
        @pl.loop(0, 8)
        def _(t):
            _, dst = exchange_refs(kind, g)
            pltpu.make_async_copy(dst, dst, a2a_recv.at[kind, t]).wait()

    def hop(number, ref, device):
        return pltpu.make_async_remote_copy(
            src_ref=ref,
            dst_ref=ref,
            send_sem=ring_send.at[number],
            recv_sem=ring_recv.at[number],
            device_id=device,
            device_id_type=MESH,
        )

    def y_next(s):
        return line(z * NY + wrap(y + s, NY))

    def z_next(s):
        return line(wrap(z + s, NZ) * NY + y)

    def near(i):
        return wrap(z + (-((i + 1) // 2) if i % 2 else i // 2), NZ)

    def early_y(step, s):
        if step == 1:
            ref = kv.at[0, z, y]
        else:
            ref = kv.at[0, z, wrap(y - s, NY), 0 if s == 1 else 1]
        return hop(2 * (step - 1) + (s == 1), ref, y_next(s))

    def early_first(n, s):
        ref = kv.at[0, z, lax.rem(y + (0, 3, 1, 2)[n], NY)]
        return hop(18 + 2 * n + (s == 1), ref, z_next(s))

    def early_z(step, s):
        ref = kv.at[0, wrap(z - s * (step - 1), NZ)]
        if step == 4:
            ref = kv.at[0, wrap(z - s * (step - 1), NZ), :, 0 if s == 1 else 1]
        return hop(4 + 2 * (step - 2) + (s == 1), ref, z_next(s))

    def late_z(step, s):
        ref = kv.at[1, wrap(z - s * (step - 1), NZ), y]
        return hop(10 + 2 * (step - 1) + (s == 1), ref, z_next(s))

    def late_first(i, s):
        return hop(26 + 2 * i + (s == 1), kv.at[1, near(i), y], y_next(s))

    def late_second(i, s):
        ref = kv.at[1, near(i), wrap(y - s, NY), 0 if s == 1 else 1]
        return hop(42 + 2 * i + (s == 1), ref, y_next(s))

    def ways(family, step):
        return (-1,) if family in (late_z,) and step == 4 else (1, -1)

    def begin(family, *steps):
        for step in steps:
            for s in ways(family, step):
                family(step, s).start()

    def arrived(family, *steps):
        for step in steps:
            for s in ways(family, step):
                family(step, s).wait_recv()

    def left(family, *steps):
        for step in steps:
            for s in ways(family, step):
                family(step, s).wait_send()

    def halo_plane(e):
        return pltpu.make_async_remote_copy(
            src_ref=lkv.at[e, SPAN],
            dst_ref=lkv.at[jnp.where(z == NZ - 1, 1 - e, e), 0],
            send_sem=halo_send.at[e],
            recv_sem=halo_recv.at[jnp.where(z == NZ - 1, 1 - e, e)],
            device_id=z_next(1),
            device_id_type=MESH,
        )

    def halo_side(number, landing, source, target, s):
        return pltpu.make_async_remote_copy(
            src_ref=lkv.at[:, source],
            dst_ref=lkv.at[:, target],
            send_sem=halo_send.at[number],
            recv_sem=halo_recv.at[landing],
            device_id=y_next(s),
            device_id_type=MESH,
        )

    def halo_up():
        return halo_side(2, 2, jnp.where(y == NY - 1, 0, SPAN), SPAN - 1, 1)

    def halo_down():
        return halo_side(3, 3, jnp.where(y == 0, SPAN, 0), SPAN - 3, -1)

    def halo_on(s):
        return halo_side(4 + (s == 1), 4, SPAN - 1 if s == 1 else SPAN - 3, SPAN - 2, s)

    inner = (y == 1) | (y == 2)

    def halo_1():
        for e in range(2):
            halo_plane(e).start()
        pl.when(y != NY - 1)(lambda: halo_up().start())
        pl.when(y == 0)(lambda: halo_down().start())

    def halo_2():
        for e in range(2):
            halo_plane(e).wait_recv()
        pl.when(y == NY - 1)(lambda: halo_up().start())
        pl.when(y != 0)(lambda: halo_down().start())

    def halo_3():
        halo_up().wait_recv()
        halo_down().wait_recv()

        @pl.when(inner)
        def _():
            halo_on(1).start()
            halo_on(-1).start()

    def normalized(x):
        x = x.astype(jnp.float32)
        r = x * cos_ref[...] + pltpu.roll(x, HEAD // 2, 1) * sin_ref[...]
        mean = jnp.mean(r * r, axis=-1, keepdims=True)
        return (r * lax.rsqrt(mean + norm_epsilon)).astype(jnp.bfloat16)

    send(KG)
    send(VG)
    load_c.wait()
    load_s.wait()
    cos_ref[...] = tiled(cos_half[...], 2)
    sin_ref[...] = jnp.concatenate([-sin_half[...], sin_half[...]], axis=1)
    load_k.wait()
    for h in range(8):
        cols = slice(h * HEAD, (h + 1) * HEAD)
        nk[:, cols] = normalized(kl_ref[:, cols])
    load_q.wait()

    @pl.loop(0, 8)
    def _(t):
        for h in range(GROUP):
            cols = pl.ds(pl.multiple_of(t * WIDE + h * HEAD, HEAD), HEAD)
            nq[:, cols] = normalized(ql_ref[:, cols])

    received(KG)
    received(VG)
    begin(late_z, 1)
    begin(early_y, 1)
    begin(early_first, 0)
    begin(late_first, 0)
    send(QG)
    m_ref[...] = jnp.full(m_ref.shape, masked_score, jnp.float32)
    acc[...] = jnp.zeros(acc.shape, jnp.float32)
    load_l.wait()

    @pl.loop(0, 2)
    def _(e):
        first = 8 * HEAD + (32 * e + c - SPAN) * TOK
        wide = jnp.concatenate(
            [labels[pl.ds(first // HEAD + n, 1), :] for n in range(9)], axis=1
        ).astype(jnp.float32)
        shifted = pltpu.roll(wide, 9 * HEAD - HEAD // 2, 1)
        wide = jnp.where(lax.rem(c, 2) == 1, shifted, wide)
        own = wide[:, SPAN * TOK : 8 * HEAD]
        row = lax.broadcasted_iota(jnp.int32, (TOK, 2 * HEAD), 0)
        col = lax.broadcasted_iota(jnp.int32, (TOK, 2 * HEAD), 1)
        mine = jnp.sum(jnp.where(row == col, own, 0.0), axis=1, keepdims=True)
        row_pos = lax.broadcasted_iota(jnp.int32, (TOK, KEYS), 0) + SPAN * TOK
        key_pos = lax.broadcasted_iota(jnp.int32, (TOK, KEYS), 1)
        allowed = (wide[:, :KEYS] == mine) & (key_pos <= row_pos)
        bias[e] = jnp.where(allowed, 0.0, masked_score)

    arrived(early_y, 1)
    begin(early_y, 2)
    begin(early_first, 1, 2)
    arrived(late_z, 1)
    begin(late_z, 2)
    begin(late_first, 1, 2)
    arrived(early_y, 2)
    begin(early_first, 3)
    send(KL)
    send(VL)
    arrived(late_z, 2)
    begin(late_z, 3)
    begin(late_first, 3, 4)
    received(QG)

    @pl.loop(0, 2)
    def _(e):
        block = e * 32 + c
        pos = block * TOK + lax.broadcasted_iota(jnp.int32, (TOK, HEAD), 0)
        level = lax.shift_right_logical(pos + 1, temper_shift) + 1
        temper = 1.0 + temper_slope * jnp.log(level.astype(jnp.float32))
        factor = temper * (scaling * log2e)
        for h in range(GROUP):
            x = qg_buf[e, :, h * HEAD : (h + 1) * HEAD].astype(jnp.float32) * factor
            high = x.astype(jnp.bfloat16)
            low = (x - high.astype(jnp.float32)).astype(jnp.bfloat16)
            qs[e, h * TOK : (h + 1) * TOK, :] = jnp.concatenate([high, low], axis=1)

    def local_attention():
        received(QL)
        halo_on(1).wait_recv()

        @pl.loop(0, 2)
        def _(e):
            k = lkv[e, :, 0].reshape(KEYS, HEAD)
            v = lkv[e, :, 1].reshape(KEYS, HEAD)
            va = jnp.concatenate([v, jnp.ones((KEYS, HEAD), jnp.bfloat16)], axis=1)
            for h in range(GROUP):
                cols = slice(h * HEAD, (h + 1) * HEAD)
                s = lax.dot_general(
                    lq_buf[e, :, cols], k, (((1,), (1,)), ((), ())),
                    preferred_element_type=jnp.float32,
                )
                p = jnp.exp2(s * (scaling * log2e) + bias[e]).astype(jnp.bfloat16)
                o = jnp.dot(p, va, preferred_element_type=jnp.float32)
                ol_buf[e, :, cols] = (o[:, :HEAD] / o[:, HEAD:]).astype(jnp.bfloat16)

        send(OL)

    def unit(eq, ek, zs, ys, start=None, slope=None):
        keys = TOK * len(zs)
        k = jnp.concatenate([kv[ek, a, b, 0] for a, b in zip(zs, ys)], axis=0)
        v = jnp.concatenate([kv[ek, a, b, 1] for a, b in zip(zs, ys)], axis=0)
        kk = jnp.concatenate([k, k], axis=1)
        va = jnp.concatenate([v, jnp.ones((keys, HEAD), jnp.bfloat16)], axis=1)

        def scores(t):
            return lax.dot_general(
                qs[eq, t * TILE : (t + 1) * TILE, :], kk, (((1,), (1,)), ((), ())),
                preferred_element_type=jnp.float32,
            )

        ahead = scores(0)
        for t in range(ROWS // TILE):
            rows = pl.ds(t * TILE, TILE)
            s = ahead
            if t + 1 < ROWS // TILE:
                ahead = scores(t + 1)
            if start is not None:
                r = t * TILE + lax.broadcasted_iota(jnp.int32, (TILE, HEAD), 0)
                for h in range(GROUP - 1, 0, -1):
                    r = jnp.where(r >= h * TOK, r - h * TOK, r)
                limit = tiled(r * slope + (start - (keys - CHUNK)), CHUNK // HEAD)
                key = lax.broadcasted_iota(jnp.int32, (TILE, CHUNK), 1)
                last = jnp.where(key <= limit, s[:, keys - CHUNK :], masked_score)
                s = last if keys == CHUNK else jnp.concatenate([s[:, : keys - CHUNK], last], 1)
            before = m_ref[eq, rows, :]
            peak = jnp.maximum(before, jnp.max(s, axis=1, keepdims=True))
            factor = jnp.exp2(before - peak)
            p = jnp.exp2(s - tiled(peak, keys // HEAD)).astype(jnp.bfloat16)
            acc[eq, rows, :] = acc[eq, rows, :] * tiled(factor, 2) + jnp.dot(
                p, va, preferred_element_type=jnp.float32
            )
            m_ref[eq, rows, :] = peak

    def finish(e):
        for h in range(GROUP):
            o = acc[e, h * TOK : (h + 1) * TOK, :]
            og_buf[e, :, h * HEAD : (h + 1) * HEAD] = (o[:, :HEAD] / o[:, HEAD:]).astype(
                jnp.bfloat16
            )
        send_global(e)

    def service_1():
        arrived(late_z, 3)
        begin(late_z, 4)
        begin(late_first, 5, 6)
        arrived(early_first, 0, 1, 2, 3)
        begin(early_z, 2)
        received(KL)
        received(VL)
        halo_1()
        send(QL)

    def service_2():
        arrived(late_z, 4)
        begin(late_first, 7)
        halo_2()

    def service_3():
        for i in range(5):
            arrived(late_first, i)
            begin(late_second, i)

    def service_4():
        arrived(early_z, 2)
        begin(early_z, 3)
        for i in range(5, 8):
            arrived(late_first, i)
            begin(late_second, i)
        halo_3()

    def service_8():
        arrived(early_z, 3)
        begin(early_z, 4)
        local_attention()

    def service_10():
        arrived(early_z, 4)

    def service_11():
        finish(0)
        arrived(late_second, *range(8))

    services = {
        2: service_1,
        3: service_2,
        4: service_3,
        6: service_4,
        12: service_8,
        14: service_10,
        16: service_11,
    }

    @pl.loop(0, 17)
    def _(j):
        slot = j // 2
        second = lax.rem(j, 2) == 1
        for place, action in services.items():
            pl.when(j == place)(action)

        column = (slot == 2) | (slot == 4) | (slot == 5) | (slot == 8)
        far = jnp.where(slot < 2, slot, jnp.where(slot == 3, 2, slot - 3))
        below = lax.rem(z - far + NZ, NZ)
        above = lax.rem(z + far, NZ)
        turn = jnp.where(slot == 2, 0, jnp.where(slot == 4, 3, jnp.where(slot == 5, 1, 2)))
        y_col = lax.rem(y + turn, NY)

        two = (far > 0) & (far < 4)
        wide = jnp.where(column, z >= 4, two & (jnp.logical_not(second) | (z + far >= NZ)))
        do = jnp.where(column, jnp.logical_not(second), jnp.logical_not(second) | (z >= far))
        masked = column | (second & (far == 0))
        eq = jnp.where(jnp.logical_not(column) & second, 0, 1)
        ek = jnp.where(column, 1, 0)
        slope = jnp.where(column & (y_col != y), 0, 1)
        start = jnp.where(
            column,
            z * TOK + jnp.where(y_col < y, TOK - 1, jnp.where(y_col == y, 0, -1)),
            y * TOK,
        )
        zs = [jnp.where(column, n, below if n < 4 else above) for n in range(8)]
        ys = [jnp.where(column, y_col, n % 4) for n in range(8)]
        free = jnp.logical_not(masked)
        narrow = jnp.logical_not(wide)

        @pl.when(do & narrow & free)
        def _():
            unit(eq, ek, zs[:4], ys[:4])

        @pl.when(do & narrow & masked)
        def _():
            unit(eq, ek, zs[:4], ys[:4], start, slope)

        @pl.when(do & wide & free)
        def _():
            unit(eq, ek, zs, ys)

        @pl.when(do & wide & masked)
        def _():
            unit(eq, ek, zs, ys, start, slope)

    finish(1)
    for kind in (KG, VG, KL, VL, QL, QG, OL):
        sent(kind)
    left(early_y, 1, 2)
    left(early_first, 0, 1, 2, 3)
    left(early_z, 2, 3, 4)
    left(late_z, 1, 2, 3, 4)
    left(late_first, *range(8))
    left(late_second, *range(8))
    for e in range(2):
        halo_plane(e).wait_send()
    halo_up().wait_send()
    halo_down().wait_send()

    @pl.when(inner)
    def _():
        halo_on(1).wait_send()
        halo_on(-1).wait_send()

    received(OL)
    received(OG)
    sent(OG)


def shards(
    query_local, key_local, value_local, stretch_labels, query_global, key_global, value_global
):
    ctx = lax.axis_index("ctx")
    head = lax.axis_index("head")
    positions = (ctx * TOK + head * OWN + jnp.arange(OWN, dtype=jnp.int32)).astype(jnp.float32)
    half = HEAD // 2
    frequency = rope_base ** (-(jnp.arange(half, dtype=jnp.float32) * 2.0 / HEAD))
    angles = positions[:, None] * frequency[None, :]
    cosine, sine = jnp.cos(angles), jnp.sin(angles)
    any_space = pl.BlockSpec(memory_space=pl.ANY)
    bf16, f32 = jnp.bfloat16, jnp.float32
    out = jax.ShapeDtypeStruct(query_local.shape, bf16)
    return pl.pallas_call(
        kernel,
        out_shape=(out, out),
        in_specs=[any_space] * 9,
        out_specs=(any_space, any_space),
        scratch_shapes=[
            pltpu.VMEM((OWN, 8 * WIDE), bf16),
            pltpu.VMEM((OWN, 8 * HEAD), bf16),
            pltpu.VMEM((OWN, HEAD // 2), f32),
            pltpu.VMEM((OWN, HEAD // 2), f32),
            pltpu.VMEM((OWN, HEAD), f32),
            pltpu.VMEM((OWN, HEAD), f32),
            pltpu.VMEM((112, HEAD), jnp.int32),
            pltpu.VMEM((2, NZ, NY, 2, TOK, HEAD), bf16),
            pltpu.VMEM((2, SPAN + 1, 2, TOK, HEAD), bf16),
            pltpu.VMEM((2, TOK, WIDE), bf16),
            pltpu.VMEM((2, TOK, WIDE), bf16),
            pltpu.VMEM((OWN, 8 * WIDE), bf16),
            pltpu.VMEM((OWN, 8 * HEAD), bf16),
            pltpu.VMEM((2, ROWS, 2 * HEAD), bf16),
            pltpu.VMEM((2, ROWS, HEAD), f32),
            pltpu.VMEM((2, ROWS, 2 * HEAD), f32),
            pltpu.VMEM((2, TOK, WIDE), bf16),
            pltpu.VMEM((2, TOK, WIDE), bf16),
            pltpu.VMEM((2, TOK, KEYS), f32),
            pltpu.SemaphoreType.DMA((8, 8)),
            pltpu.SemaphoreType.DMA((8, 8)),
            pltpu.SemaphoreType.DMA((58,)),
            pltpu.SemaphoreType.DMA((58,)),
            pltpu.SemaphoreType.DMA((6,)),
            pltpu.SemaphoreType.DMA((5,)),
            pltpu.SemaphoreType.DMA((5,)),
        ],
        compiler_params=pltpu.CompilerParams(
            collective_id=0, has_side_effects=True, vmem_limit_bytes=62 << 20
        ),
    )(
        query_local, key_local, value_local, query_global, key_global, value_global,
        cosine, sine, stretch_labels.reshape(-1, HEAD),
    )


def solution(mesh):
    rows = P(("ctx", "head"), None)
    return jax.shard_map(
        shards,
        mesh=mesh,
        in_specs=(rows, rows, rows, P(), rows, rows, rows),
        out_specs=(rows, rows),
        check_vma=False,
    )
```
